32 devices in a mesh: groups: 2 (over y), date: 8 (over z, x), strip: 2 (over core).
Axes of the slice: x: 2, y: 2, z: 4, core: 2. Of those that a mesh axis runs over, the one named last changes fastest.
Arguments:
- slc_tiles: float32 [2, 16, 32, 1024], P(None, ('groups', 'date'), None, 'strip'), parts along dimension 1, may hold values from -6 to 6
- coreg_shift: int32 [16, 2], P(('groups', 'date')), parts along dimension 0, may hold values from -16 to 16, as said below
- center_freq: float32 [16], P('groups'), parts along dimension 0, may hold values from -0.2 to 0.2
- filter_taps: float32 [17], replicated, may hold values from 0.05 to 0.4
- owner_table: int32 [16], P('groups'), parts along dimension 0, may hold values from 0 to 7, each once
Outputs:
- phases: float32 [2, 16, 8192], P(None, 'groups', ('date', 'strip')), parts along dimension 1
The draws below stay inside these ranges and needn't reach their ends.
There are 2 independent parts, one for each index of `groups`. The reference program is written for one: setup_inputs(seed, part) draws one part's arguments, and reference() takes and returns one part's arrays. A program takes and returns all parts, laid end to end along the dimension named above; an argument that names none is the same for every part. Nothing has to cross between parts.
Inputs may be any that keep to these rules, and one draw needn't show every extreme that they name: `coreg_shift`: both 16 and -16 occur in every draw. `owner_table`: a permutation: every index of date owns exactly one block.
All inputs are finite; a program needn't handle non-finite values.
Results may differ from the reference program's by a relative error of at most 0.0003.
Values sent between devices are 32-bit elements; how exact they have to be, the bound alone decides.
No kernel may reach another device: no remote copies, remote signals or barrier semaphores. Data moves between devices by JAX's collectives and lax.ppermute only.
A program may use at most 64 MiB of HBM per device.

```python
import jax
import jax.numpy as jnp
from jax import lax

LINES = 32
STRIP_COLS = 512
LB = 16
SMAX = 16
TAPS = 17
ROUNDS = 3
MINI = 8
ITERS = 3
DATES = 8
RANGE = 1024
LBLK = 2
PIXELS = 8192
N_DATE = 8
N_STRIP = 2


def draw_coreg_shift(key, part):
    key_values, key_high, key_low = jax.random.split(key, 3)
    total_cells = DATES * LBLK
    values = jax.random.randint(key_values, (total_cells,), -SMAX, SMAX + 1, dtype=jnp.int32)
    spot_high = jax.random.randint(key_high, (), 0, total_cells, dtype=jnp.int32)
    spot_low = (spot_high + 1 + jax.random.randint(key_low, (), 0, total_cells - 1, dtype=jnp.int32)) % total_cells
    values = values.at[spot_high].set(SMAX).at[spot_low].set(-SMAX)
    return values.reshape(DATES, LBLK)


def steps_of(own_key, extent, cuts, least, top_value):
    gain, own = 1.0, jax.random.fold_in(own_key, 6)
    for dim, shards_of in cuts:
        heights = jnp.exp(jax.random.uniform(jax.random.fold_in(own, dim), (shards_of,), jnp.float32, least / len(cuts), top_value / len(cuts)))
        gain = gain * jnp.repeat(heights, extent[dim] // shards_of).reshape([-1 if axis == dim else 1 for axis in range(len(extent))])
    return gain


def bell_draw(rng, dims, spread, bound, cuts=(), held_as=jnp.bfloat16):
    gain = steps_of(rng, dims, cuts, -0.22, 0.18) if cuts else 1.0
    values = jax.random.normal(rng, dims, jnp.float32) * spread * gain
    return jnp.minimum(jnp.maximum(values, -bound), bound).astype(held_as)


def setup_inputs(seed: int = 0, part: int = 0) -> dict:
    arg_keys = jax.random.split(jax.random.key(seed), 6)
    part_splits = jax.random.split(jax.random.fold_in(arg_keys[5], part), 6)
    return {
        "slc_tiles": bell_draw(part_splits[0], (2, DATES, LINES, RANGE), 0.6, 6.0, ((1, 8), (3, 2)), jnp.float32),
        "coreg_shift": draw_coreg_shift(jax.random.fold_in(jax.random.fold_in(arg_keys[5], part), 71), part),
        "center_freq": jnp.clip(jax.random.uniform(part_splits[2], (DATES,), jnp.float32, -0.2, 0.2), -0.2, 0.2),
        "filter_taps": jnp.clip(jax.random.uniform(arg_keys[3], (TAPS,), jnp.float32, 0.05, 0.4), 0.05, 0.4),
        "owner_table": jax.random.permutation(part_splits[4], N_DATE).astype(jnp.int32),
    }


def look_mean(field):
    layout = field.shape
    folded = field.reshape(layout[:-2] + (layout[-2] // 2, 2, layout[-1] // 2, 2))
    return lax.optimization_barrier(jnp.sum(folded, axis=(-3, -1))) * 0.25

def partner_view(field, stride):
    layout = field.shape
    folded = field.reshape((layout[0] // (2 * stride), 2, stride) + layout[1:])
    return jnp.flip(folded, axis=1).reshape(layout)

def pair_terms(lower_re, lower_im, stride):
    layout = lower_re.shape
    folded_re = lower_re.reshape((layout[0] // stride, stride) + layout[1:])
    folded_im = lower_im.reshape((layout[0] // stride, stride) + layout[1:])
    full_shape = (2 * layout[0],) + layout[1:]
    terms_re = jnp.stack([folded_re, folded_re], axis=1).reshape(full_shape)
    terms_im = jnp.stack([folded_im, -folded_im], axis=1).reshape(full_shape)
    return (terms_re, terms_im)

def link_phase(intensity, pair_list):
    vec_re = jnp.ones_like(intensity)
    vec_im = jnp.zeros_like(intensity)
    layout = intensity.shape
    for sweep_step in range(ITERS):
        next_re = intensity * vec_re
        next_im = intensity * vec_im
        for terms_re, terms_im, stride in pair_list:
            other_re = partner_view(vec_re, stride)
            other_im = partner_view(vec_im, stride)
            next_re = next_re + terms_re * other_re - terms_im * other_im
            next_im = next_im + terms_re * other_im + terms_im * other_re
        energy = (next_re * next_re + next_im * next_im).reshape((layout[0] // MINI, MINI) + layout[1:])
        length = jnp.sqrt(lax.optimization_barrier(jnp.sum(energy, axis=1, keepdims=True)))
        factor = jnp.broadcast_to(1.0 / jnp.maximum(length, 1.0), energy.shape).reshape(layout)
        vec_re = next_re * factor
        vec_im = next_im * factor
    return (vec_re, vec_im)

def tap_pair(filter_taps, rotation):
    angle = rotation[:, None] * (jnp.arange(TAPS, dtype=jnp.float32)[None, :] - TAPS // 2)
    return (filter_taps[None, :] * jnp.cos(angle), filter_taps[None, :] * jnp.sin(angle))

def band_filter_ref(slices, tap_re, tap_im):
    out_cols = slices.shape[-1] - 2 * (TAPS // 2)
    acc_re = jnp.zeros((slices.shape[0], slices.shape[2], out_cols), jnp.float32)
    acc_im = jnp.zeros((slices.shape[0], slices.shape[2], out_cols), jnp.float32)
    for t in range(TAPS):
        seg_re = slices[:, 0, :, t:t + out_cols]
        seg_im = slices[:, 1, :, t:t + out_cols]
        c_re = tap_re[:, t][:, None, None]
        c_im = tap_im[:, t][:, None, None]
        acc_re = acc_re + c_re * seg_re - c_im * seg_im
        acc_im = acc_im + c_re * seg_im + c_im * seg_re
    return (acc_re, acc_im)

def reference(slc_tiles, coreg_shift, center_freq, filter_taps, owner_table):
    tap_reach = TAPS // 2
    margin = SMAX + tap_reach
    dates_first = jnp.transpose(slc_tiles, (1, 0, 2, 3))
    padded = jnp.pad(dates_first, ((0, 0), (0, 0), (0, 0), (margin, margin)))
    line_shift = jnp.repeat(coreg_shift, LB, axis=1)
    full_width = RANGE + 2 * tap_reach

    def resample_one(pair_args):
        picture, shifts = pair_args
        column_index = jnp.arange(full_width, dtype=jnp.int32)[None, :] + SMAX + shifts[:, None].astype(jnp.int32)
        column_index = jnp.broadcast_to(column_index[None], (2,) + column_index.shape)
        return jnp.take_along_axis(picture, column_index, axis=2)
    resampled = lax.map(resample_one, (padded, line_shift))
    centre = resampled[:, :, :, tap_reach:tap_reach + RANGE]
    intensity = look_mean(centre[:, 0] * centre[:, 0] + centre[:, 1] * centre[:, 1])
    date_ids = jnp.arange(DATES, dtype=jnp.int32)
    pair_list = []
    for round_bit in range(ROUNDS):
        stride = 1 << round_bit
        lower_ids = date_ids.reshape(DATES // (2 * stride), 2, stride)[:, 0, :].reshape(-1)
        upper_ids = lower_ids + stride
        rotation = jnp.pi * (center_freq[upper_ids] - center_freq[lower_ids])
        low_re, low_im = tap_pair(filter_taps, rotation)
        high_re, high_im = tap_pair(filter_taps, -rotation)
        first_re, first_im = band_filter_ref(resampled[lower_ids], low_re, low_im)
        second_re, second_im = band_filter_ref(resampled[upper_ids], high_re, high_im)
        ifg_re = look_mean(first_re * second_re + first_im * second_im)
        ifg_im = look_mean(first_im * second_re - first_re * second_im)
        terms_re, terms_im = pair_terms(ifg_re, ifg_im, stride)
        pair_list.append((terms_re, terms_im, stride))
    vec_re, vec_im = link_phase(intensity, pair_list)
    result = jnp.stack([vec_re, vec_im])
    quarter = LINES // 4
    strip_half = STRIP_COLS // 2
    block_len = quarter * strip_half // N_DATE
    arranged = result.reshape(2, DATES, 2, quarter, N_STRIP, strip_half)
    arranged = jnp.transpose(arranged, (0, 1, 4, 2, 3, 5)).reshape(2, DATES, N_STRIP, 2, N_DATE, block_len)
    inverse = jnp.zeros((N_DATE,), jnp.int32).at[owner_table].set(jnp.arange(N_DATE, dtype=jnp.int32))
    chosen = jnp.take(arranged, inverse, axis=4)
    chosen = jnp.transpose(chosen, (0, 1, 4, 2, 3, 5))
    return chosen.reshape(2, DATES, PIXELS)
```

```python
import functools

import jax
import jax.numpy as jnp
from jax import lax
from jax.experimental import pallas as pl
from jax.experimental.pallas import tpu as pltpu
from jax.sharding import PartitionSpec as P

SMAX = 16
TAPS = 17
ROUNDS = 3
MINI = 8
ITERS = 3
LANES = 128
REACH = TAPS // 2
VMEM_LIMIT = 16 * 1024 * 1024


def smem():
    return pl.BlockSpec(memory_space=pltpu.SMEM)


def vmem():
    return pl.BlockSpec(memory_space=pltpu.VMEM)


def params():
    return pltpu.CompilerParams(vmem_limit_bytes=VMEM_LIMIT)


def coef_kernel(freq_ref, out_ref):
    date = lax.broadcasted_iota(jnp.int32, (MINI, LANES), 0)
    lane = lax.broadcasted_iota(jnp.int32, (MINI, LANES), 1)

    def freq_of(index):
        total = jnp.zeros((MINI, LANES), jnp.float32)
        for d in range(MINI):
            total = jnp.where(index == d, freq_ref[d], total)
        return total

    own = freq_of(date)
    rotation = jnp.zeros((MINI, LANES), jnp.float32)
    for r in range(ROUNDS):
        q = jnp.pi * (freq_of(jnp.bitwise_xor(date, 1 << r)) - own)
        rotation = jnp.where(lane // REACH == r, q, rotation)
    angle = rotation * (lane % REACH + 1).astype(jnp.float32)
    cosine, sine = jnp.cos(angle), jnp.sin(angle)
    for j in range(ROUNDS * REACH):
        out_ref[2 * j] = jnp.broadcast_to(cosine[:, j : j + 1], (MINI, LANES))
        out_ref[2 * j + 1] = jnp.broadcast_to(sine[:, j : j + 1], (MINI, LANES))


def pack_kernel(slot_ref, shift_ref, place_ref, own_ref, other_ref, out_ref):
    _, rows, cols = own_ref.shape
    blocks = shift_ref.shape[1]
    block_rows = rows // blocks
    share = block_rows // MINI
    height = 2 * blocks * share
    first = place_ref[0] == 0
    for e in range(blocks):
        offset = LANES - REACH + shift_ref[0, e]
        for c in range(2):
            lines = pl.ds(e * block_rows, block_rows)
            left = jnp.where(first, 0.0, other_ref[c, lines, cols - LANES : cols])
            right = jnp.where(first, other_ref[c, lines, 0:LANES], 0.0)
            line = jnp.concatenate([left, own_ref[c, lines, :], right], axis=1)
            total = cols + 2 * LANES
            moved = pltpu.roll(line, total - offset, 1)
            for q in range(MINI):
                for b in range(out_ref.shape[1] // height):
                    row = b * height + (c * blocks + e) * share
                    out_ref[slot_ref[q], row : row + share, :] = moved[
                        q * share : (q + 1) * share, b * LANES : (b + 1) * LANES
                    ]


def partner(value, stride):
    if 2 * stride == MINI:
        return pltpu.roll(value, stride, 0)
    date = lax.broadcasted_iota(jnp.int32, value.shape, 0)
    up = pltpu.roll(value, MINI - stride, 0)
    down = pltpu.roll(value, stride, 0)
    return jnp.where((date // stride) % 2 == 0, up, down)


def link_kernel(tap_ref, coef_ref, data_ref, out_ref, look_ref):
    blocks = 2
    nb = 2 * out_ref.shape[2] // blocks // LANES
    height = 4 * blocks
    stride = (nb + 1) * height
    lane = lax.broadcasted_iota(jnp.int32, (MINI, LANES), 1)
    fields = 2 * ROUNDS + 1
    half = 2 * LANES
    for e in range(blocks):
        for b in range(nb):
            sums = [None] * fields
            for p in range(2):
                pieces = []
                for c in range(2):
                    row = (c * blocks + e) * 2 + p
                    pieces.append(
                        [
                            data_ref[pl.ds((b + i) * height + row, MINI, stride=stride), :]
                            for i in range(2)
                        ]
                    )

                def at(c, t):
                    here, there = pieces[c]
                    if t == 0:
                        return here
                    both = jnp.where(lane < t, there, here)
                    return pltpu.roll(both, LANES - t, 1)

                centre = [at(c, REACH) for c in range(2)]
                acc = [[tap_ref[REACH] * centre[c] for c in range(2)] for _ in range(ROUNDS)]
                for k in range(1, REACH + 1):
                    plus = [tap_ref[REACH + k] * at(c, REACH + k) for c in range(2)]
                    minus = [tap_ref[REACH - k] * at(c, REACH - k) for c in range(2)]
                    even = [plus[c] + minus[c] for c in range(2)]
                    odd = [plus[c] - minus[c] for c in range(2)]
                    for r in range(ROUNDS):
                        j = r * REACH + k - 1
                        cosine, sine = coef_ref[2 * j], coef_ref[2 * j + 1]
                        acc[r][0] = acc[r][0] + (cosine * even[0] - sine * odd[1])
                        acc[r][1] = acc[r][1] + (cosine * even[1] + sine * odd[0])
                terms = []
                for r in range(ROUNDS):
                    y_re, y_im = acc[r]
                    z_re, z_im = partner(y_re, 1 << r), partner(y_im, 1 << r)
                    terms.append(y_re * z_re + y_im * z_im)
                    terms.append(y_im * z_re - y_re * z_im)
                terms.append(centre[0] * centre[0] + centre[1] * centre[1])
                sums = [t if s is None else s + t for s, t in zip(sums, terms)]
            for f in range(fields):
                row = ((e * nb + b) // 2 * fields + f) * MINI
                look_ref[row : row + MINI, pl.ds(b % 2 * LANES, LANES)] = sums[f]
    value = look_ref[...]
    source = lax.broadcasted_iota(jnp.int32, (half, LANES), 0)
    target = lax.broadcasted_iota(jnp.int32, (half, LANES), 1)
    weights = jnp.where(source // 2 == target, 0.25, 0.0).astype(jnp.bfloat16)
    looked = jnp.zeros((value.shape[0], LANES), jnp.float32)
    for _ in range(3):
        part = value.astype(jnp.bfloat16)
        value = value - part.astype(jnp.float32)
        looked = looked + jnp.dot(part, weights, preferred_element_type=jnp.float32)
    for g in range(blocks * nb // 2):
        base = g * fields * MINI
        field = [looked[base + f * MINI : base + (f + 1) * MINI] for f in range(fields)]
        vec_re = jnp.ones((MINI, LANES), jnp.float32)
        vec_im = jnp.zeros((MINI, LANES), jnp.float32)
        for _ in range(ITERS):
            next_re = field[-1] * vec_re
            next_im = field[-1] * vec_im
            for r in range(ROUNDS):
                o_re, o_im = partner(vec_re, 1 << r), partner(vec_im, 1 << r)
                t_re, t_im = field[2 * r], field[2 * r + 1]
                next_re = next_re + t_re * o_re - t_im * o_im
                next_im = next_im + t_re * o_im + t_im * o_re
            energy = jnp.sum(next_re * next_re + next_im * next_im, axis=0, keepdims=True)
            factor = 1.0 / jnp.maximum(jnp.sqrt(energy), 1.0)
            vec_re = next_re * factor
            vec_im = next_im * factor
        out_ref[0, :, pl.ds(g * LANES, LANES)] = vec_re
        out_ref[1, :, pl.ds(g * LANES, LANES)] = vec_im


def to_owners(linked, inverse, blocks):
    date_count = lax.axis_size("date")
    position = lax.axis_index("date")
    parts = date_count // MINI
    member = position % MINI
    cut = linked.reshape(2, MINI, blocks, parts, -1)
    own_blocks = lax.dynamic_slice_in_dim(jnp.argsort(inverse), member * parts, parts)
    outgoing = jnp.zeros((date_count, 2, MINI, blocks, cut.shape[-1]), jnp.float32)
    outgoing = outgoing.at[own_blocks].set(jnp.moveaxis(cut, 3, 0))
    arrived = lax.all_to_all(outgoing, "date", split_axis=0, concat_axis=0, tiled=True)
    source = inverse[position] // parts
    arrived = arrived.reshape((parts, MINI) + arrived.shape[1:])
    chosen = lax.dynamic_index_in_dim(arrived, source, axis=1, keepdims=False)
    return jnp.moveaxis(chosen, 1, 0).reshape(2, date_count, -1)


def shards(slc_tiles, coreg_shift, center_freq, filter_taps, owner_table):
    own_tile = slc_tiles[:, 0]
    _, rows, cols = own_tile.shape
    date_count = lax.axis_size("date")
    strips = lax.axis_size("strip")
    blocks = coreg_shift.shape[1]
    share = rows // blocks // MINI
    position = lax.axis_index("date")
    other_tile = lax.ppermute(own_tile, "strip", [(s, strips - 1 - s) for s in range(strips)])
    if date_count == MINI:
        slots, stack, freq = owner_table, None, center_freq
    else:
        slots = jnp.arange(MINI, dtype=jnp.int32)
        stack = [list(range(g, g + MINI)) for g in range(0, date_count, MINI)]
        freq = lax.dynamic_slice_in_dim(center_freq, position // MINI * MINI, MINI)
    coefs = pl.pallas_call(
        coef_kernel,
        out_shape=jax.ShapeDtypeStruct((2 * ROUNDS * REACH, MINI, LANES), jnp.float32),
        in_specs=[smem()],
        out_specs=vmem(),
        compiler_params=params(),
        name="coefs",
    )(freq)
    height = 2 * blocks * share * (cols // LANES + 1)
    packed = pl.pallas_call(
        pack_kernel,
        out_shape=jax.ShapeDtypeStruct((MINI, height, LANES), jnp.float32),
        in_specs=[smem(), smem(), smem(), vmem(), vmem()],
        out_specs=vmem(),
        compiler_params=params(),
        name="pack",
    )(slots, coreg_shift, lax.axis_index("strip")[None], own_tile, other_tile)
    data = lax.all_to_all(
        packed, "date", split_axis=0, concat_axis=0, axis_index_groups=stack, tiled=True
    )
    pixels = blocks * share // 2 * cols // 2
    fields = 2 * ROUNDS + 1
    linked = pl.pallas_call(
        link_kernel,
        out_shape=jax.ShapeDtypeStruct((2, MINI, pixels), jnp.float32),
        in_specs=[smem(), vmem(), vmem()],
        out_specs=vmem(),
        scratch_shapes=[pltpu.VMEM((pixels // LANES * fields * MINI, 2 * LANES), jnp.float32)],
        compiler_params=params(),
        name="link",
    )(filter_taps, coefs, data.reshape(-1, LANES))
    if date_count == MINI:
        return linked
    date_ids = jnp.arange(date_count, dtype=jnp.int32)
    inverse = jnp.zeros((date_count,), jnp.int32).at[owner_table].set(date_ids)
    return to_owners(linked, inverse, blocks)


def solution(mesh):
    in_specs = (
        P(None, ("groups", "date"), None, "strip"),
        P(("groups", "date"), None),
        P("groups"),
        P(),
        P("groups"),
    )
    out_specs = P(None, "groups", ("date", "strip"))
    return jax.shard_map(shards, mesh=mesh, in_specs=in_specs, out_specs=out_specs, check_vma=False)
```

```python
import jax
import jax.numpy as jnp
from jax import lax
from jax.experimental import pallas as pl
from jax.experimental.pallas import tpu as pltpu
from jax.sharding import PartitionSpec as P

SMAX = 16
TAPS = 17
ROUNDS = 3
MINI = 8
ITERS = 3
LANES = 128
REACH = TAPS // 2
VMEM_LIMIT = 16 * 1024 * 1024


def vmem():
    return pl.BlockSpec(memory_space=pltpu.VMEM)


def hbm():
    return pl.BlockSpec(memory_space=pltpu.HBM)


def in_hbm(value):
    return pltpu.with_memory_space_constraint(value, pltpu.HBM)


def params():
    return pltpu.CompilerParams(vmem_limit_bytes=VMEM_LIMIT)


def prep_kernel(
    freq_hbm, tap_hbm, slot_hbm, shift_hbm, tile_hbm,
    coef_ref, tap_out, slot_out, shift_out, packed_ref,
    freq_ref, tap_ref, slot_ref, shift_ref, tile_ref, sems,
):
    copies = [
        pltpu.make_async_copy(source, target, sems.at[i])
        for i, (source, target) in enumerate(
            (
                (freq_hbm, freq_ref),
                (shift_hbm, shift_ref),
                (slot_hbm, slot_ref),
                (tap_hbm, tap_ref),
                (tile_hbm, tile_ref),
            )
        )
    ]
    for copy in copies:
        copy.start()
    date = lax.broadcasted_iota(jnp.int32, (MINI, LANES), 0)
    lane = lax.broadcasted_iota(jnp.int32, (MINI, LANES), 1)
    for copy in copies[:4]:
        copy.wait()

    def freq_of(index):
        total = jnp.zeros((MINI, LANES), jnp.float32)
        for d in range(MINI):
            total = jnp.where(index == d, freq_ref[d], total)
        return total

    own = freq_of(date)
    rotation = jnp.zeros((MINI, LANES), jnp.float32)
    for r in range(ROUNDS):
        q = jnp.pi * (freq_of(jnp.bitwise_xor(date, 1 << r)) - own)
        rotation = jnp.where(lane // REACH == r, q, rotation)
    angle = rotation * (lane % REACH + 1).astype(jnp.float32)
    cosine, sine = jnp.cos(angle), jnp.sin(angle)
    for j in range(ROUNDS * REACH):
        coef_ref[2 * j] = jnp.broadcast_to(cosine[:, j : j + 1], (MINI, LANES))
        coef_ref[2 * j + 1] = jnp.broadcast_to(sine[:, j : j + 1], (MINI, LANES))
    for t in range(TAPS):
        tap_out[t] = jnp.full((MINI, LANES), tap_ref[t], jnp.float32)
    for q in range(MINI):
        slot_out[q] = jnp.full((MINI, LANES), slot_ref[q], jnp.int32)
    _, rows, cols = tile_ref.shape
    blocks = shift_ref.shape[1]
    block_rows = rows // blocks
    share = block_rows // MINI
    height = 2 * blocks * share
    row = lax.broadcasted_iota(jnp.int32, (MINI, LANES), 0)
    offsets = jnp.zeros((MINI, LANES), jnp.int32)
    for e in range(blocks):
        offsets = jnp.where(row // share % blocks == e, shift_ref[0, e] + SMAX, offsets)
        shift_out[e] = jnp.full((MINI, LANES), shift_ref[0, e] + SMAX, jnp.int32)
    shift_out[blocks] = offsets
    copies[4].wait()
    total = cols + 2 * LANES
    for e in range(blocks):
        offset = LANES - REACH + shift_ref[0, e]
        for c in range(2):
            rim = jnp.zeros((block_rows, LANES), jnp.float32)
            lines = tile_ref[c, e * block_rows : (e + 1) * block_rows, :]
            moved = pltpu.roll(jnp.concatenate([rim, lines, rim], axis=1), total - offset, 1)
            for q in range(MINI):
                for b in range(packed_ref.shape[1] // height):
                    at = b * height + (c * blocks + e) * share
                    packed_ref[slot_ref[q], at : at + share, :] = moved[
                        q * share : (q + 1) * share, b * LANES : (b + 1) * LANES
                    ]


def rim_kernel(place_ref, slot_ref, shift_ref, other_ref, packed_ref, out_ref):
    _, rows, cols = other_ref.shape
    blocks = shift_ref.shape[0] - 1
    block_rows = rows // blocks
    share = block_rows // MINI
    first = place_ref[0] == 0
    lane = lax.broadcasted_iota(jnp.int32, (MINI, LANES), 1)
    reach = SMAX + REACH
    moved = []
    for c in range(2):
        for e in range(blocks):
            lines = pl.ds(e * block_rows, block_rows)
            rim = jnp.where(first, other_ref[c, lines, 0:LANES], other_ref[c, lines, cols - LANES : cols])
            shift = jnp.concatenate([shift_ref[e]] * (block_rows // MINI), axis=0)
            for bit in range((2 * SMAX).bit_length()):
                rim = jnp.where(shift & (1 << bit) != 0, pltpu.roll(rim, LANES - (1 << bit), 1), rim)
            moved.append(pltpu.roll(rim, reach, 1))
    pieces = [
        jnp.concatenate([m[q * share : (q + 1) * share] for m in moved], axis=0) for q in range(MINI)
    ]
    edge = reach - shift_ref[blocks]
    height = 2 * blocks * share
    last = cols // LANES
    side = jnp.where(first, 0, 1)
    masks = {
        0: lane + (1 - side) * 2 * LANES < edge,
        last - 1: lane - side * 4 * LANES >= edge + LANES,
        last: lane - side * 4 * LANES >= edge,
    }
    for j in range(MINI):
        rim = pieces[0]
        for q in range(1, MINI):
            rim = jnp.where(slot_ref[q] == j, pieces[q], rim)
        for b, mask in masks.items():
            at = slice(b * height, (b + 1) * height)
            out_ref[j, at, :] = jnp.where(mask, rim, packed_ref[j, at, :])


def partner(value, stride):
    if 2 * stride == MINI:
        return pltpu.roll(value, stride, 0)
    date = lax.broadcasted_iota(jnp.int32, value.shape, 0)
    up = pltpu.roll(value, MINI - stride, 0)
    down = pltpu.roll(value, stride, 0)
    return jnp.where((date // stride) % 2 == 0, up, down)


def link_kernel(tap_ref, coef_ref, data_ref, out_ref):
    blocks = 2
    nb = 2 * out_ref.shape[2] // blocks // LANES
    height = 4 * blocks
    stride = (nb + 1) * height
    lane = lax.broadcasted_iota(jnp.int32, (MINI, LANES), 1)
    fields = 2 * ROUNDS + 1
    source = lax.broadcasted_iota(jnp.int32, (2 * LANES, LANES), 0)
    target = lax.broadcasted_iota(jnp.int32, (2 * LANES, LANES), 1)
    weights = jnp.where(source // 2 == target, 0.25, 0.0).astype(jnp.bfloat16)

    def sums_of(e, b):
        sums = [None] * fields
        for p in range(2):
            pieces = []
            for c in range(2):
                row = (c * blocks + e) * 2 + p
                pieces.append(
                    [data_ref[pl.ds((b + i) * height + row, MINI, stride=stride), :] for i in range(2)]
                )

            def at(c, t):
                here, there = pieces[c]
                if t == 0:
                    return here
                return pltpu.roll(jnp.where(lane < t, there, here), LANES - t, 1)

            centre = [at(c, REACH) for c in range(2)]
            acc = [[tap_ref[REACH] * centre[c] for c in range(2)] for _ in range(ROUNDS)]
            for k in range(1, REACH + 1):
                plus = [tap_ref[REACH + k] * at(c, REACH + k) for c in range(2)]
                minus = [tap_ref[REACH - k] * at(c, REACH - k) for c in range(2)]
                even = [plus[c] + minus[c] for c in range(2)]
                odd = [plus[c] - minus[c] for c in range(2)]
                for r in range(ROUNDS):
                    j = r * REACH + k - 1
                    cosine, sine = coef_ref[2 * j], coef_ref[2 * j + 1]
                    acc[r][0] = acc[r][0] + (cosine * even[0] - sine * odd[1])
                    acc[r][1] = acc[r][1] + (cosine * even[1] + sine * odd[0])
            terms = []
            for r in range(ROUNDS):
                y_re, y_im = acc[r]
                z_re, z_im = partner(y_re, 1 << r), partner(y_im, 1 << r)
                terms.append(y_re * z_re + y_im * z_im)
                terms.append(y_im * z_re - y_re * z_im)
            terms.append(centre[0] * centre[0] + centre[1] * centre[1])
            sums = [t if s is None else s + t for s, t in zip(sums, terms)]
        return jnp.concatenate(sums, axis=0)

    for g in range(blocks * nb // 2):
        e, b = g // (nb // 2), g % (nb // 2) * 2
        value = jnp.concatenate([sums_of(e, b), sums_of(e, b + 1)], axis=1)
        looked = jnp.zeros((value.shape[0], LANES), jnp.float32)
        for _ in range(3):
            part = value.astype(jnp.bfloat16)
            value = value - part.astype(jnp.float32)
            looked = looked + jnp.dot(part, weights, preferred_element_type=jnp.float32)
        field = [looked[f * MINI : (f + 1) * MINI] for f in range(fields)]
        vec_re = jnp.ones((MINI, LANES), jnp.float32)
        vec_im = jnp.zeros((MINI, LANES), jnp.float32)
        for _ in range(ITERS):
            next_re = field[-1] * vec_re
            next_im = field[-1] * vec_im
            for r in range(ROUNDS):
                o_re, o_im = partner(vec_re, 1 << r), partner(vec_im, 1 << r)
                t_re, t_im = field[2 * r], field[2 * r + 1]
                next_re = next_re + t_re * o_re - t_im * o_im
                next_im = next_im + t_re * o_im + t_im * o_re
            energy = jnp.sum(next_re * next_re + next_im * next_im, axis=0, keepdims=True)
            factor = 1.0 / jnp.maximum(jnp.sqrt(energy), 1.0)
            vec_re = next_re * factor
            vec_im = next_im * factor
        out_ref[0, :, pl.ds(g * LANES, LANES)] = vec_re
        out_ref[1, :, pl.ds(g * LANES, LANES)] = vec_im


def to_owners(linked, inverse, blocks):
    date_count = lax.axis_size("date")
    position = lax.axis_index("date")
    parts = date_count // MINI
    member = position % MINI
    cut = linked.reshape(2, MINI, blocks, parts, -1)
    own_blocks = lax.dynamic_slice_in_dim(jnp.argsort(inverse), member * parts, parts)
    outgoing = jnp.zeros((date_count, 2, MINI, blocks, cut.shape[-1]), jnp.float32)
    outgoing = outgoing.at[own_blocks].set(jnp.moveaxis(cut, 3, 0))
    arrived = lax.all_to_all(outgoing, "date", split_axis=0, concat_axis=0, tiled=True)
    source = inverse[position] // parts
    arrived = arrived.reshape((parts, MINI) + arrived.shape[1:])
    chosen = lax.dynamic_index_in_dim(arrived, source, axis=1, keepdims=False)
    return jnp.moveaxis(chosen, 1, 0).reshape(2, date_count, -1)


def shards(slc_tiles, coreg_shift, center_freq, filter_taps, owner_table):
    own_tile = slc_tiles[:, 0]
    _, rows, cols = own_tile.shape
    date_count = lax.axis_size("date")
    strips = lax.axis_size("strip")
    blocks = coreg_shift.shape[1]
    share = rows // blocks // MINI
    position = lax.axis_index("date")
    other_tile = lax.ppermute(own_tile, "strip", [(s, strips - 1 - s) for s in range(strips)])
    if date_count == MINI:
        slots, stack, freq = owner_table, None, center_freq
    else:
        slots = jnp.arange(MINI, dtype=jnp.int32)
        stack = [list(range(g, g + MINI)) for g in range(0, date_count, MINI)]
        freq = lax.dynamic_slice_in_dim(center_freq, position // MINI * MINI, MINI)
    tall = 2 * blocks * share
    height = tall * (cols // LANES + 1)
    tile = (MINI, LANES)
    coefs, taps, slot_marks, shift_marks, packed = pl.pallas_call(
        prep_kernel,
        out_shape=(
            jax.ShapeDtypeStruct((2 * ROUNDS * REACH,) + tile, jnp.float32),
            jax.ShapeDtypeStruct((TAPS,) + tile, jnp.float32),
            jax.ShapeDtypeStruct((MINI,) + tile, jnp.int32),
            jax.ShapeDtypeStruct((blocks + 1,) + tile, jnp.int32),
            jax.ShapeDtypeStruct((MINI, height, LANES), jnp.float32),
        ),
        in_specs=[hbm()] * 5,
        out_specs=(vmem(),) * 5,
        scratch_shapes=[
            pltpu.SMEM(freq.shape, jnp.float32),
            pltpu.SMEM(filter_taps.shape, jnp.float32),
            pltpu.SMEM(slots.shape, jnp.int32),
            pltpu.SMEM(coreg_shift.shape, jnp.int32),
            pltpu.VMEM(own_tile.shape, jnp.float32),
            pltpu.SemaphoreType.DMA((5,)),
        ],
        compiler_params=params(),
        name="prep",
    )(*(in_hbm(x) for x in (freq, filter_taps, slots, coreg_shift, own_tile)))
    packed = pl.pallas_call(
        rim_kernel,
        out_shape=jax.ShapeDtypeStruct(packed.shape, jnp.float32),
        in_specs=[pl.BlockSpec(memory_space=pltpu.SMEM)] + [vmem()] * 4,
        out_specs=vmem(),
        input_output_aliases={4: 0},
        compiler_params=params(),
        name="rim",
    )(lax.axis_index("strip")[None], slot_marks, shift_marks, other_tile, packed)
    data = lax.all_to_all(
        packed, "date", split_axis=0, concat_axis=0, axis_index_groups=stack, tiled=True
    )
    linked = pl.pallas_call(
        link_kernel,
        out_shape=jax.ShapeDtypeStruct((2, MINI, blocks * share // 2 * cols // 2), jnp.float32),
        in_specs=[vmem()] * 3,
        out_specs=vmem(),
        compiler_params=params(),
        name="link",
    )(taps, coefs, data.reshape(-1, LANES))
    if date_count == MINI:
        return linked
    date_ids = jnp.arange(date_count, dtype=jnp.int32)
    inverse = jnp.zeros((date_count,), jnp.int32).at[owner_table].set(date_ids)
    return to_owners(linked, inverse, blocks)


def solution(mesh):
    in_specs = (
        P(None, ("groups", "date"), None, "strip"),
        P(("groups", "date"), None),
        P("groups"),
        P(),
        P("groups"),
    )
    out_specs = P(None, "groups", ("date", "strip"))
    return jax.shard_map(shards, mesh=mesh, in_specs=in_specs, out_specs=out_specs, check_vma=False)
```

```python
import jax
import jax.numpy as jnp
from jax import lax
from jax.experimental import pallas as pl
from jax.experimental.pallas import tpu as pltpu
from jax.sharding import PartitionSpec as P

SMAX = 16
TAPS = 17
ROUNDS = 3
MINI = 8
ITERS = 3
LANES = 128
REACH = TAPS // 2
ORDER = (4, 7, 5, 6, 0, 2, 1, 3)
VMEM_LIMIT = 16 * 1024 * 1024


def vmem():
    return pl.BlockSpec(memory_space=pltpu.VMEM)


def hbm():
    return pl.BlockSpec(memory_space=pltpu.HBM)


def in_hbm(value):
    return pltpu.with_memory_space_constraint(value, pltpu.HBM)


def params():
    return pltpu.CompilerParams(vmem_limit_bytes=VMEM_LIMIT)


def prep_kernel(
    freq_hbm, tap_hbm, slot_hbm, shift_hbm, tile_hbm,
    coef_ref, tap_out, slot_out, shift_out, packed_ref,
    freq_ref, tap_ref, slot_ref, shift_ref, tile_ref, sems,
):
    copies = [
        pltpu.make_async_copy(source, target, sems.at[i])
        for i, (source, target) in enumerate(
            (
                (freq_hbm, freq_ref),
                (shift_hbm, shift_ref),
                (slot_hbm, slot_ref),
                (tap_hbm, tap_ref),
                (tile_hbm, tile_ref),
            )
        )
    ]
    for copy in copies:
        copy.start()
    date = lax.broadcasted_iota(jnp.int32, (MINI, LANES), 0)
    lane = lax.broadcasted_iota(jnp.int32, (MINI, LANES), 1)
    for copy in copies[:4]:
        copy.wait()
    slots = []
    for q in range(MINI):
        slot = jnp.int32(0)
        for place, member in enumerate(ORDER):
            slot = jnp.where(slot_ref[q] == member, place, slot)
        slots.append(slot)

    def freq_of(index):
        total = jnp.zeros((MINI, LANES), jnp.float32)
        for d in range(MINI):
            total = jnp.where(index == d, freq_ref[d], total)
        return total

    own = freq_of(date)
    rotation = jnp.zeros((MINI, LANES), jnp.float32)
    for r in range(ROUNDS):
        q = jnp.pi * (freq_of(jnp.bitwise_xor(date, 1 << r)) - own)
        rotation = jnp.where(lane // REACH == r, q, rotation)
    angle = rotation * (lane % REACH + 1).astype(jnp.float32)
    cosine, sine = jnp.cos(angle), jnp.sin(angle)
    for j in range(ROUNDS * REACH):
        coef_ref[2 * j] = jnp.broadcast_to(cosine[:, j : j + 1], (MINI, LANES))
        coef_ref[2 * j + 1] = jnp.broadcast_to(sine[:, j : j + 1], (MINI, LANES))
    for t in range(TAPS):
        tap_out[t] = jnp.full((MINI, LANES), tap_ref[t], jnp.float32)
    for q in range(MINI):
        slot_out[q] = jnp.full((MINI, LANES), slots[q], jnp.int32)
    _, rows, cols = tile_ref.shape
    blocks = shift_ref.shape[1]
    block_rows = rows // blocks
    share = block_rows // MINI
    height = 2 * blocks * share
    row = lax.broadcasted_iota(jnp.int32, (MINI, LANES), 0)
    offsets = jnp.zeros((MINI, LANES), jnp.int32)
    for e in range(blocks):
        offsets = jnp.where(row // share % blocks == e, shift_ref[0, e] + SMAX, offsets)
        shift_out[e] = jnp.full((MINI, LANES), shift_ref[0, e] + SMAX, jnp.int32)
    shift_out[blocks] = offsets
    copies[4].wait()
    total = cols + 2 * LANES
    for e in range(blocks):
        offset = LANES - REACH + shift_ref[0, e]
        for c in range(2):
            rim = jnp.zeros((block_rows, LANES), jnp.float32)
            lines = tile_ref[c, e * block_rows : (e + 1) * block_rows, :]
            moved = pltpu.roll(jnp.concatenate([rim, lines, rim], axis=1), total - offset, 1)
            for q in range(MINI):
                for b in range(packed_ref.shape[1] // height):
                    at = b * height + (c * blocks + e) * share
                    packed_ref[slots[q], at : at + share, :] = moved[
                        q * share : (q + 1) * share, b * LANES : (b + 1) * LANES
                    ]


def rim_kernel(slot_ref, shift_ref, other_ref, packed_ref, out_ref):
    _, rows, cols = other_ref.shape
    blocks = shift_ref.shape[0] - 1
    block_rows = rows // blocks
    share = block_rows // MINI
    first = lax.axis_index("strip") == 0
    lane = lax.broadcasted_iota(jnp.int32, (MINI, LANES), 1)
    reach = SMAX + REACH
    moved = []
    for c in range(2):
        for e in range(blocks):
            lines = pl.ds(e * block_rows, block_rows)
            rim = jnp.where(first, other_ref[c, lines, 0:LANES], other_ref[c, lines, cols - LANES : cols])
            source = jnp.concatenate([(lane - reach + shift_ref[e]) & (LANES - 1)] * (block_rows // MINI), axis=0)
            moved.append(jnp.take_along_axis(rim, source, axis=1))
    pieces = [
        jnp.concatenate([m[q * share : (q + 1) * share] for m in moved], axis=0) for q in range(MINI)
    ]
    edge = reach - shift_ref[blocks]
    height = 2 * blocks * share
    last = cols // LANES
    side = jnp.where(first, 0, 1)
    masks = {
        0: lane + (1 - side) * 2 * LANES < edge,
        last - 1: lane - side * 4 * LANES >= edge + LANES,
        last: lane - side * 4 * LANES >= edge,
    }
    for j in range(MINI):
        rim = pieces[0]
        for q in range(1, MINI):
            rim = jnp.where(slot_ref[q] == j, pieces[q], rim)
        for b, mask in masks.items():
            at = slice(b * height, (b + 1) * height)
            out_ref[j, at, :] = jnp.where(mask, rim, packed_ref[j, at, :])


def partner(value, stride):
    if 2 * stride == MINI:
        return pltpu.roll(value, stride, 0)
    date = lax.broadcasted_iota(jnp.int32, value.shape, 0)
    up = pltpu.roll(value, MINI - stride, 0)
    down = pltpu.roll(value, stride, 0)
    return jnp.where((date // stride) % 2 == 0, up, down)


def link_kernel(tap_ref, coef_ref, data_ref, out_ref):
    blocks = 2
    nb = 2 * out_ref.shape[2] // blocks // LANES
    height = 4 * blocks
    stride = (nb + 1) * height
    lane = lax.broadcasted_iota(jnp.int32, (MINI, LANES), 1)
    fields = 2 * ROUNDS + 1
    source = lax.broadcasted_iota(jnp.int32, (2 * LANES, LANES), 0)
    target = lax.broadcasted_iota(jnp.int32, (2 * LANES, LANES), 1)
    weights = jnp.where(source // 2 == target, 0.25, 0.0).astype(jnp.bfloat16)

    date = lax.broadcasted_iota(jnp.int32, (MINI, LANES), 0)
    place_of = jnp.zeros((MINI, LANES), jnp.int32)
    for place, member in enumerate(ORDER):
        place_of = jnp.where(date == member, place, place_of)

    def load(row):
        arrived = data_ref[pl.ds(row, MINI, stride=stride), :]
        return jnp.take_along_axis(arrived, place_of, axis=0)

    def sums_of(e, b):
        sums = [None] * fields
        for p in range(2):
            pieces = []
            for c in range(2):
                row = (c * blocks + e) * 2 + p
                pieces.append([load((b + i) * height + row) for i in range(2)])

            def at(c, t):
                here, there = pieces[c]
                if t == 0:
                    return here
                return pltpu.roll(jnp.where(lane < t, there, here), LANES - t, 1)

            centre = [at(c, REACH) for c in range(2)]
            acc = [[tap_ref[REACH] * centre[c] for c in range(2)] for _ in range(ROUNDS)]
            for k in range(1, REACH + 1):
                plus = [tap_ref[REACH + k] * at(c, REACH + k) for c in range(2)]
                minus = [tap_ref[REACH - k] * at(c, REACH - k) for c in range(2)]
                even = [plus[c] + minus[c] for c in range(2)]
                odd = [plus[c] - minus[c] for c in range(2)]
                for r in range(ROUNDS):
                    j = r * REACH + k - 1
                    cosine, sine = coef_ref[2 * j], coef_ref[2 * j + 1]
                    acc[r][0] = acc[r][0] + (cosine * even[0] - sine * odd[1])
                    acc[r][1] = acc[r][1] + (cosine * even[1] + sine * odd[0])
            terms = []
            for r in range(ROUNDS):
                y_re, y_im = acc[r]
                z_re, z_im = partner(y_re, 1 << r), partner(y_im, 1 << r)
                terms.append(y_re * z_re + y_im * z_im)
                terms.append(y_im * z_re - y_re * z_im)
            terms.append(centre[0] * centre[0] + centre[1] * centre[1])
            sums = [t if s is None else s + t for s, t in zip(sums, terms)]
        return jnp.concatenate(sums, axis=0)

    for g in range(blocks * nb // 2):
        e, b = g // (nb // 2), g % (nb // 2) * 2
        value = jnp.concatenate([sums_of(e, b), sums_of(e, b + 1)], axis=1)
        looked = jnp.zeros((value.shape[0], LANES), jnp.float32)
        for _ in range(3):
            part = value.astype(jnp.bfloat16)
            value = value - part.astype(jnp.float32)
            looked = looked + jnp.dot(part, weights, preferred_element_type=jnp.float32)
        field = [looked[f * MINI : (f + 1) * MINI] for f in range(fields)]
        vec_re = jnp.ones((MINI, LANES), jnp.float32)
        vec_im = jnp.zeros((MINI, LANES), jnp.float32)
        for _ in range(ITERS):
            next_re = field[-1] * vec_re
            next_im = field[-1] * vec_im
            for r in range(ROUNDS):
                o_re, o_im = partner(vec_re, 1 << r), partner(vec_im, 1 << r)
                t_re, t_im = field[2 * r], field[2 * r + 1]
                next_re = next_re + t_re * o_re - t_im * o_im
                next_im = next_im + t_re * o_im + t_im * o_re
            energy = jnp.sum(next_re * next_re + next_im * next_im, axis=0, keepdims=True)
            factor = 1.0 / jnp.maximum(jnp.sqrt(energy), 1.0)
            vec_re = next_re * factor
            vec_im = next_im * factor
        out_ref[0, :, pl.ds(g * LANES, LANES)] = vec_re
        out_ref[1, :, pl.ds(g * LANES, LANES)] = vec_im


def to_owners(linked, inverse, blocks):
    date_count = lax.axis_size("date")
    position = lax.axis_index("date")
    parts = date_count // MINI
    member = position % MINI
    cut = linked.reshape(2, MINI, blocks, parts, -1)
    own_blocks = lax.dynamic_slice_in_dim(jnp.argsort(inverse), member * parts, parts)
    outgoing = jnp.zeros((date_count, 2, MINI, blocks, cut.shape[-1]), jnp.float32)
    outgoing = outgoing.at[own_blocks].set(jnp.moveaxis(cut, 3, 0))
    arrived = lax.all_to_all(outgoing, "date", split_axis=0, concat_axis=0, tiled=True)
    source = inverse[position] // parts
    arrived = arrived.reshape((parts, MINI) + arrived.shape[1:])
    chosen = lax.dynamic_index_in_dim(arrived, source, axis=1, keepdims=False)
    return jnp.moveaxis(chosen, 1, 0).reshape(2, date_count, -1)


def shards(slc_tiles, coreg_shift, center_freq, filter_taps, owner_table):
    own_tile = slc_tiles[:, 0]
    _, rows, cols = own_tile.shape
    date_count = lax.axis_size("date")
    strips = lax.axis_size("strip")
    blocks = coreg_shift.shape[1]
    share = rows // blocks // MINI
    position = lax.axis_index("date")
    other_tile = lax.ppermute(own_tile, "strip", [(s, strips - 1 - s) for s in range(strips)])
    if date_count == MINI:
        slots, freq = owner_table, center_freq
    else:
        slots = jnp.arange(MINI, dtype=jnp.int32)
        freq = lax.dynamic_slice_in_dim(center_freq, position // MINI * MINI, MINI)
    tall = 2 * blocks * share
    height = tall * (cols // LANES + 1)
    tile = (MINI, LANES)
    coefs, taps, slot_marks, shift_marks, packed = pl.pallas_call(
        prep_kernel,
        out_shape=(
            jax.ShapeDtypeStruct((2 * ROUNDS * REACH,) + tile, jnp.float32),
            jax.ShapeDtypeStruct((TAPS,) + tile, jnp.float32),
            jax.ShapeDtypeStruct((MINI,) + tile, jnp.int32),
            jax.ShapeDtypeStruct((blocks + 1,) + tile, jnp.int32),
            jax.ShapeDtypeStruct((MINI, height, LANES), jnp.float32),
        ),
        in_specs=[hbm()] * 5,
        out_specs=(vmem(),) * 5,
        scratch_shapes=[
            pltpu.SMEM(freq.shape, jnp.float32),
            pltpu.SMEM(filter_taps.shape, jnp.float32),
            pltpu.SMEM(slots.shape, jnp.int32),
            pltpu.SMEM(coreg_shift.shape, jnp.int32),
            pltpu.VMEM(own_tile.shape, jnp.float32),
            pltpu.SemaphoreType.DMA((5,)),
        ],
        compiler_params=params(),
        name="prep",
    )(*(in_hbm(x) for x in (freq, filter_taps, slots, coreg_shift, own_tile)))
    packed = pl.pallas_call(
        rim_kernel,
        out_shape=jax.ShapeDtypeStruct(packed.shape, jnp.float32),
        in_specs=[vmem()] * 4,
        out_specs=vmem(),
        input_output_aliases={3: 0},
        compiler_params=params(),
        name="rim",
    )(slot_marks, shift_marks, other_tile, packed)
    stacks = [[g + member for member in ORDER] for g in range(0, date_count, MINI)]
    data = lax.all_to_all(
        packed, "date", split_axis=0, concat_axis=0, axis_index_groups=stacks, tiled=True
    )
    linked = pl.pallas_call(
        link_kernel,
        out_shape=jax.ShapeDtypeStruct((2, MINI, blocks * share // 2 * cols // 2), jnp.float32),
        in_specs=[vmem()] * 3,
        out_specs=vmem(),
        compiler_params=params(),
        name="link",
    )(taps, coefs, data.reshape(-1, LANES))
    if date_count == MINI:
        return linked
    date_ids = jnp.arange(date_count, dtype=jnp.int32)
    inverse = jnp.zeros((date_count,), jnp.int32).at[owner_table].set(date_ids)
    return to_owners(linked, inverse, blocks)


def solution(mesh):
    in_specs = (
        P(None, ("groups", "date"), None, "strip"),
        P(("groups", "date"), None),
        P("groups"),
        P(),
        P("groups"),
    )
    out_specs = P(None, "groups", ("date", "strip"))
    return jax.shard_map(shards, mesh=mesh, in_specs=in_specs, out_specs=out_specs, check_vma=False)
```

```python
import jax
import jax.numpy as jnp
from jax import lax
from jax.experimental import pallas as pl
from jax.experimental.pallas import tpu as pltpu
from jax.sharding import PartitionSpec as P

SMAX = 16
TAPS = 17
ROUNDS = 3
MINI = 8
ITERS = 3
LANES = 128
REACH = TAPS // 2
ORDER = (5, 7, 3, 4, 0, 6, 1, 2)
VMEM_LIMIT = 16 * 1024 * 1024


def vmem():
    return pl.BlockSpec(memory_space=pltpu.VMEM)


def hbm():
    return pl.BlockSpec(memory_space=pltpu.HBM)


def in_hbm(value):
    return pltpu.with_memory_space_constraint(value, pltpu.HBM)


def params():
    return pltpu.CompilerParams(vmem_limit_bytes=VMEM_LIMIT)


def prep_kernel(
    freq_hbm, tap_hbm, slot_hbm, shift_hbm, tile_hbm,
    coef_ref, tap_out, slot_out, shift_out, packed_ref,
    freq_ref, tap_ref, slot_ref, shift_ref, tile_ref, sems,
):
    copies = [
        pltpu.make_async_copy(source, target, sems.at[i])
        for i, (source, target) in enumerate(
            (
                (freq_hbm, freq_ref),
                (shift_hbm, shift_ref),
                (slot_hbm, slot_ref),
                (tap_hbm, tap_ref),
                (tile_hbm, tile_ref),
            )
        )
    ]
    for copy in copies:
        copy.start()
    date = lax.broadcasted_iota(jnp.int32, (MINI, LANES), 0)
    lane = lax.broadcasted_iota(jnp.int32, (MINI, LANES), 1)
    for copy in copies[:4]:
        copy.wait()
    slots = []
    for q in range(MINI):
        slot = jnp.int32(0)
        for place, member in enumerate(ORDER):
            slot = jnp.where(slot_ref[q] == member, place, slot)
        slots.append(slot)

    def freq_of(index):
        total = jnp.zeros((MINI, LANES), jnp.float32)
        for d in range(MINI):
            total = jnp.where(index == d, freq_ref[d], total)
        return total

    own = freq_of(date)
    rotation = jnp.zeros((MINI, LANES), jnp.float32)
    for r in range(ROUNDS):
        q = jnp.pi * (freq_of(jnp.bitwise_xor(date, 1 << r)) - own)
        rotation = jnp.where(lane // REACH == r, q, rotation)
    angle = rotation * (lane % REACH + 1).astype(jnp.float32)
    cosine, sine = jnp.cos(angle), jnp.sin(angle)
    taps = [jnp.full((MINI, LANES), tap_ref[t], jnp.float32) for t in range(TAPS)]
    for j in range(ROUNDS * REACH):
        tap = taps[REACH + 1 + j % REACH]
        coef_ref[2 * j] = tap * jnp.broadcast_to(cosine[:, j : j + 1], (MINI, LANES))
        coef_ref[2 * j + 1] = tap * jnp.broadcast_to(sine[:, j : j + 1], (MINI, LANES))
    tap_out[0] = taps[REACH]
    for k in range(1, REACH + 1):
        tap_out[k] = taps[REACH - k] / taps[REACH + k]
    for q in range(MINI):
        slot_out[q] = jnp.full((MINI, LANES), slots[q], jnp.int32)
    _, rows, cols = tile_ref.shape
    blocks = shift_ref.shape[1]
    block_rows = rows // blocks
    share = block_rows // MINI
    height = 2 * blocks * share
    row = lax.broadcasted_iota(jnp.int32, (MINI, LANES), 0)
    offsets = jnp.zeros((MINI, LANES), jnp.int32)
    for e in range(blocks):
        offsets = jnp.where(row // share % blocks == e, shift_ref[0, e] + SMAX, offsets)
        shift_out[e] = jnp.full((MINI, LANES), shift_ref[0, e] + SMAX, jnp.int32)
    shift_out[blocks] = offsets
    copies[4].wait()
    total = cols + 2 * LANES
    for e in range(blocks):
        offset = LANES - REACH + shift_ref[0, e]
        for c in range(2):
            rim = jnp.zeros((block_rows, LANES), jnp.float32)
            lines = tile_ref[c, e * block_rows : (e + 1) * block_rows, :]
            moved = pltpu.roll(jnp.concatenate([rim, lines, rim], axis=1), total - offset, 1)
            for q in range(MINI):
                for b in range(packed_ref.shape[1] // height):
                    at = b * height + (c * blocks + e) * share
                    packed_ref[slots[q], at : at + share, :] = moved[
                        q * share : (q + 1) * share, b * LANES : (b + 1) * LANES
                    ]


def rim_kernel(slot_ref, shift_ref, other_ref, packed_ref, out_ref):
    _, rows, cols = other_ref.shape
    blocks = shift_ref.shape[0] - 1
    block_rows = rows // blocks
    share = block_rows // MINI
    first = lax.axis_index("strip") == 0
    lane = lax.broadcasted_iota(jnp.int32, (MINI, LANES), 1)
    reach = SMAX + REACH
    moved = []
    for c in range(2):
        for e in range(blocks):
            lines = pl.ds(e * block_rows, block_rows)
            rim = jnp.where(first, other_ref[c, lines, 0:LANES], other_ref[c, lines, cols - LANES : cols])
            source = jnp.concatenate([(lane - reach + shift_ref[e]) & (LANES - 1)] * (block_rows // MINI), axis=0)
            moved.append(jnp.take_along_axis(rim, source, axis=1))
    pieces = [
        jnp.concatenate([m[q * share : (q + 1) * share] for m in moved], axis=0) for q in range(MINI)
    ]
    edge = reach - shift_ref[blocks]
    height = 2 * blocks * share
    last = cols // LANES
    side = jnp.where(first, 0, 1)
    masks = {
        0: lane + (1 - side) * 2 * LANES < edge,
        last - 1: lane - side * 4 * LANES >= edge + LANES,
        last: lane - side * 4 * LANES >= edge,
    }
    for j in range(MINI):
        rim = pieces[0]
        for q in range(1, MINI):
            rim = jnp.where(slot_ref[q] == j, pieces[q], rim)
        for b, mask in masks.items():
            at = slice(b * height, (b + 1) * height)
            out_ref[j, at, :] = jnp.where(mask, rim, packed_ref[j, at, :])


def partner(value, stride):
    if 2 * stride == MINI:
        return pltpu.roll(value, stride, 0)
    date = lax.broadcasted_iota(jnp.int32, value.shape, 0)
    up = pltpu.roll(value, MINI - stride, 0)
    down = pltpu.roll(value, stride, 0)
    return jnp.where((date // stride) % 2 == 0, up, down)


def link_kernel(tap_ref, coef_ref, data_ref, out_ref):
    blocks = 2
    nb = 2 * out_ref.shape[2] // blocks // LANES
    height = 4 * blocks
    stride = (nb + 1) * height
    lane = lax.broadcasted_iota(jnp.int32, (MINI, LANES), 1)
    date = lax.broadcasted_iota(jnp.int32, (MINI, LANES), 0)
    place_of = jnp.zeros((MINI, LANES), jnp.int32)
    for place, member in enumerate(ORDER):
        place_of = jnp.where(date == member, place, place_of)
    even_lane = 2 * lane % LANES

    def load(row):
        arrived = data_ref[pl.ds(row, MINI, stride=stride), :]
        return jnp.take_along_axis(arrived, place_of, axis=0)

    def sums_of(e, b):
        sums = None
        for p in range(2):
            pieces = []
            for c in range(2):
                row = (c * blocks + e) * 2 + p
                pieces.append([load((b + i) * height + row) for i in range(2)])

            def at(c, t):
                here, there = pieces[c]
                if t == 0:
                    return here
                return pltpu.roll(jnp.where(lane < t, there, here), LANES - t, 1)

            centre = [at(c, REACH) for c in range(2)]
            acc = [[tap_ref[0] * centre[c] for c in range(2)] for _ in range(ROUNDS)]
            for k in range(1, REACH + 1):
                plus = [at(c, REACH + k) for c in range(2)]
                minus = [tap_ref[k] * at(c, REACH - k) for c in range(2)]
                even = [plus[c] + minus[c] for c in range(2)]
                odd = [plus[c] - minus[c] for c in range(2)]
                for r in range(ROUNDS):
                    j = r * REACH + k - 1
                    cosine, sine = coef_ref[2 * j], coef_ref[2 * j + 1]
                    acc[r][0] = acc[r][0] + (cosine * even[0] - sine * odd[1])
                    acc[r][1] = acc[r][1] + (cosine * even[1] + sine * odd[0])
            terms = []
            for r in range(ROUNDS):
                y_re, y_im = acc[r]
                z_re, z_im = partner(y_re, 1 << r), partner(y_im, 1 << r)
                terms.append(y_re * z_re + y_im * z_im)
                terms.append(y_im * z_re - y_re * z_im)
            terms.append(centre[0] * centre[0] + centre[1] * centre[1])
            sums = terms if sums is None else [s + t for s, t in zip(sums, terms)]
        return sums

    source = lax.broadcasted_iota(jnp.int32, (2 * LANES, LANES), 0)
    target = lax.broadcasted_iota(jnp.int32, (2 * LANES, LANES), 1)
    weights = jnp.where(source // 2 == target, 0.25, 0.0).astype(jnp.bfloat16)

    def energy_of(re, im):
        return jnp.sum(re * re + im * im, axis=0, keepdims=True)

    def shrink(length):
        return 1.0 / jnp.maximum(length, 1.0)

    for g in range(blocks * nb // 2):
        e, b = g // (nb // 2), g % (nb // 2) * 2
        value = jnp.concatenate([jnp.concatenate(sums_of(e, b + i), axis=0) for i in range(2)], axis=1)
        total = jnp.zeros((value.shape[0], LANES), jnp.float32)
        for _ in range(2):
            part = value.astype(jnp.bfloat16)
            value = value - part.astype(jnp.float32)
            total = total + jnp.dot(part, weights, preferred_element_type=jnp.float32)
        field = [total[f * MINI : (f + 1) * MINI] for f in range(2 * ROUNDS + 1)]
        vec_re = field[-1] + (field[0] + field[2] + field[4])
        vec_im = field[1] + field[3] + field[5]
        energies = [energy_of(vec_re, vec_im)]
        for _ in range(1, ITERS):
            next_re = field[-1] * vec_re
            next_im = field[-1] * vec_im
            for r in range(ROUNDS):
                o_re, o_im = partner(vec_re, 1 << r), partner(vec_im, 1 << r)
                t_re, t_im = field[2 * r], field[2 * r + 1]
                next_re = next_re + (t_re * o_re - t_im * o_im)
                next_im = next_im + (t_re * o_im + t_im * o_re)
            vec_re, vec_im = next_re, next_im
            energies.append(energy_of(vec_re, vec_im))
        factor = 1.0
        for energy in energies:
            factor = factor * shrink(jnp.sqrt(energy) * factor)
        out_ref[0, :, pl.ds(g * LANES, LANES)] = vec_re * factor
        out_ref[1, :, pl.ds(g * LANES, LANES)] = vec_im * factor


def to_owners(linked, inverse, blocks):
    date_count = lax.axis_size("date")
    position = lax.axis_index("date")
    parts = date_count // MINI
    member = position % MINI
    cut = linked.reshape(2, MINI, blocks, parts, -1)
    own_blocks = lax.dynamic_slice_in_dim(jnp.argsort(inverse), member * parts, parts)
    outgoing = jnp.zeros((date_count, 2, MINI, blocks, cut.shape[-1]), jnp.float32)
    outgoing = outgoing.at[own_blocks].set(jnp.moveaxis(cut, 3, 0))
    arrived = lax.all_to_all(outgoing, "date", split_axis=0, concat_axis=0, tiled=True)
    source = inverse[position] // parts
    arrived = arrived.reshape((parts, MINI) + arrived.shape[1:])
    chosen = lax.dynamic_index_in_dim(arrived, source, axis=1, keepdims=False)
    return jnp.moveaxis(chosen, 1, 0).reshape(2, date_count, -1)


def shards(slc_tiles, coreg_shift, center_freq, filter_taps, owner_table):
    own_tile = slc_tiles[:, 0]
    _, rows, cols = own_tile.shape
    date_count = lax.axis_size("date")
    strips = lax.axis_size("strip")
    blocks = coreg_shift.shape[1]
    share = rows // blocks // MINI
    position = lax.axis_index("date")
    other_tile = lax.ppermute(own_tile, "strip", [(s, strips - 1 - s) for s in range(strips)])
    if date_count == MINI:
        slots, freq = owner_table, center_freq
    else:
        slots = jnp.arange(MINI, dtype=jnp.int32)
        freq = lax.dynamic_slice_in_dim(center_freq, position // MINI * MINI, MINI)
    tall = 2 * blocks * share
    height = tall * (cols // LANES + 1)
    tile = (MINI, LANES)
    coefs, taps, slot_marks, shift_marks, packed = pl.pallas_call(
        prep_kernel,
        out_shape=(
            jax.ShapeDtypeStruct((2 * ROUNDS * REACH,) + tile, jnp.float32),
            jax.ShapeDtypeStruct((REACH + 1,) + tile, jnp.float32),
            jax.ShapeDtypeStruct((MINI,) + tile, jnp.int32),
            jax.ShapeDtypeStruct((blocks + 1,) + tile, jnp.int32),
            jax.ShapeDtypeStruct((MINI, height, LANES), jnp.float32),
        ),
        in_specs=[hbm()] * 5,
        out_specs=(vmem(),) * 5,
        scratch_shapes=[
            pltpu.SMEM(freq.shape, jnp.float32),
            pltpu.SMEM(filter_taps.shape, jnp.float32),
            pltpu.SMEM(slots.shape, jnp.int32),
            pltpu.SMEM(coreg_shift.shape, jnp.int32),
            pltpu.VMEM(own_tile.shape, jnp.float32),
            pltpu.SemaphoreType.DMA((5,)),
        ],
        compiler_params=params(),
        name="prep",
    )(*(in_hbm(x) for x in (freq, filter_taps, slots, coreg_shift, own_tile)))
    packed = pl.pallas_call(
        rim_kernel,
        out_shape=jax.ShapeDtypeStruct(packed.shape, jnp.float32),
        in_specs=[vmem()] * 4,
        out_specs=vmem(),
        input_output_aliases={3: 0},
        compiler_params=params(),
        name="rim",
    )(slot_marks, shift_marks, other_tile, packed)
    stacks = [[g + member for member in ORDER] for g in range(0, date_count, MINI)]
    data = lax.all_to_all(
        packed, "date", split_axis=0, concat_axis=0, axis_index_groups=stacks, tiled=True
    )
    linked = pl.pallas_call(
        link_kernel,
        out_shape=jax.ShapeDtypeStruct((2, MINI, blocks * share // 2 * cols // 2), jnp.float32),
        in_specs=[vmem()] * 3,
        out_specs=vmem(),
        compiler_params=params(),
        name="link",
    )(taps, coefs, data.reshape(-1, LANES))
    if date_count == MINI:
        return linked
    date_ids = jnp.arange(date_count, dtype=jnp.int32)
    inverse = jnp.zeros((date_count,), jnp.int32).at[owner_table].set(date_ids)
    return to_owners(linked, inverse, blocks)


def solution(mesh):
    in_specs = (
        P(None, ("groups", "date"), None, "strip"),
        P(("groups", "date"), None),
        P("groups"),
        P(),
        P("groups"),
    )
    out_specs = P(None, "groups", ("date", "strip"))
    return jax.shard_map(shards, mesh=mesh, in_specs=in_specs, out_specs=out_specs, check_vma=False)
```

```python
import jax
import jax.numpy as jnp
from jax import lax
from jax.experimental import pallas as pl
from jax.experimental.pallas import tpu as pltpu
from jax.sharding import PartitionSpec as P

SMAX = 16
TAPS = 17
ROUNDS = 3
MINI = 8
ITERS = 3
LANES = 128
REACH = TAPS // 2
ORDER = (5, 7, 3, 4, 0, 6, 1, 2)
VMEM_LIMIT = 16 * 1024 * 1024


def vmem():
    return pl.BlockSpec(memory_space=pltpu.VMEM)


def hbm():
    return pl.BlockSpec(memory_space=pltpu.HBM)


def in_hbm(value):
    return pltpu.with_memory_space_constraint(value, pltpu.HBM)


def params():
    return pltpu.CompilerParams(vmem_limit_bytes=VMEM_LIMIT)


def sources(shift, lane, cols):
    first = [LANES - REACH - SMAX + shift + 2 * lane + odd for odd in range(2)]
    piece = [f >> (LANES.bit_length() - 1) for f in first]
    count = cols // LANES
    index = [2 * h + piece[odd] for odd in range(2) for h in range(count // 2)]
    index.append(jnp.where(lane < LANES // 2, count + piece[0], count - 1 + piece[1]))
    return [f & (LANES - 1) for f in first], index


def prep_kernel(
    freq_hbm, tap_hbm, slot_hbm, shift_hbm, tile_hbm,
    coef_ref, tap_out, slot_out, shift_out, packed_ref,
    freq_ref, tap_ref, slot_ref, shift_ref, tile_ref, sems,
):
    copies = [
        pltpu.make_async_copy(source, target, sems.at[i])
        for i, (source, target) in enumerate(
            (
                (freq_hbm, freq_ref),
                (shift_hbm, shift_ref),
                (slot_hbm, slot_ref),
                (tap_hbm, tap_ref),
                (tile_hbm, tile_ref),
            )
        )
    ]
    for copy in copies:
        copy.start()
    date = lax.broadcasted_iota(jnp.int32, (MINI, LANES), 0)
    lane = lax.broadcasted_iota(jnp.int32, (MINI, LANES), 1)
    for copy in copies[:4]:
        copy.wait()
    slots = []
    for q in range(MINI):
        slot = jnp.int32(0)
        for place, member in enumerate(ORDER):
            slot = jnp.where(slot_ref[q] == member, place, slot)
        slots.append(slot)

    def freq_of(index):
        total = jnp.zeros((MINI, LANES), jnp.float32)
        for d in range(MINI):
            total = jnp.where(index == d, freq_ref[d], total)
        return total

    own = freq_of(date)
    rotation = jnp.zeros((MINI, LANES), jnp.float32)
    for r in range(ROUNDS):
        q = jnp.pi * (freq_of(jnp.bitwise_xor(date, 1 << r)) - own)
        rotation = jnp.where(lane // REACH == r, q, rotation)
    angle = rotation * (lane % REACH + 1).astype(jnp.float32)
    cosine, sine = jnp.cos(angle), jnp.sin(angle)
    taps = [jnp.full((MINI, LANES), tap_ref[t], jnp.float32) for t in range(TAPS)]
    for j in range(ROUNDS * REACH):
        tap = taps[REACH + 1 + j % REACH]
        coef_ref[2 * j] = tap * jnp.broadcast_to(cosine[:, j : j + 1], (MINI, LANES))
        coef_ref[2 * j + 1] = tap * jnp.broadcast_to(sine[:, j : j + 1], (MINI, LANES))
    tap_out[0] = taps[REACH]
    for k in range(1, REACH + 1):
        tap_out[k] = taps[REACH - k] / taps[REACH + k]
    for q in range(MINI):
        slot_out[q] = jnp.full((MINI, LANES), slots[q], jnp.int32)
    _, rows, cols = tile_ref.shape
    blocks = shift_ref.shape[1]
    block_rows = rows // blocks
    share = block_rows // MINI
    height = 2 * blocks * share
    row = lax.broadcasted_iota(jnp.int32, (MINI, LANES), 0)
    offsets = jnp.zeros((MINI, LANES), jnp.int32)
    for e in range(blocks):
        offsets = jnp.where(row // share % blocks == e, shift_ref[0, e] + SMAX, offsets)
        shift_out[e] = jnp.full((MINI, LANES), shift_ref[0, e] + SMAX, jnp.int32)
    shift_out[blocks] = offsets
    count = cols // LANES
    tall_lane = lax.broadcasted_iota(jnp.int32, (block_rows, LANES), 1)
    plans = [sources(shift_ref[0, e] + SMAX, tall_lane, cols) for e in range(blocks)]
    copies[4].wait()
    for e in range(blocks):
        lanes, index = plans[e]
        for c in range(2):
            lines = pl.ds(e * block_rows, block_rows)
            taken = [
                [
                    jnp.take_along_axis(tile_ref[c, lines, v * LANES : (v + 1) * LANES], lanes[odd], axis=1)
                    for v in range(count)
                ]
                for odd in range(2)
            ]
            for b in range(count + 1):
                value = jnp.zeros((block_rows, LANES), jnp.float32)
                low = count if b == count else b % (count // 2) * 2
                for v in range(max(low, 1), min(low + 3, count) + 1):
                    if b == count:
                        source = jnp.where(tall_lane < LANES // 2, taken[0][v - 1], taken[1][v - 1])
                    else:
                        source = taken[b // (count // 2)][v - 1]
                    value = jnp.where(index[b] == v, source, value)
                at = b * height + c * blocks * share + e * share
                for q in range(MINI):
                    packed_ref[slots[q], at : at + share, :] = value[q * share : (q + 1) * share]


def rim_kernel(slot_ref, shift_ref, other_ref, packed_ref, out_ref):
    _, rows, cols = other_ref.shape
    blocks = shift_ref.shape[0] - 1
    block_rows = rows // blocks
    share = block_rows // MINI
    height = 2 * blocks * share
    count = cols // LANES
    first = lax.axis_index("strip") == 0
    lane = lax.broadcasted_iota(jnp.int32, (MINI, LANES), 1)
    tall_lane = lax.broadcasted_iota(jnp.int32, (block_rows, LANES), 1)
    moved = []
    for c in range(2):
        for e in range(blocks):
            lines = pl.ds(e * block_rows, block_rows)
            rim = jnp.where(first, other_ref[c, lines, 0:LANES], other_ref[c, lines, cols - LANES : cols])
            shift = jnp.concatenate([shift_ref[e]] * (block_rows // MINI), axis=0)
            lanes, _ = sources(shift, tall_lane, cols)
            moved.append([jnp.take_along_axis(rim, lanes[odd], axis=1) for odd in range(2)])
    pieces = [
        [jnp.concatenate([m[odd][q * share : (q + 1) * share] for m in moved], axis=0) for q in range(MINI)]
        for odd in range(2)
    ]
    _, index = sources(shift_ref[blocks], lane, cols)
    wanted = jnp.where(first, count + 1, 0)
    masks = [piece == wanted for piece in index]
    for j in range(MINI):
        rims = [pieces[odd][0] for odd in range(2)]
        for q in range(1, MINI):
            hit = slot_ref[q] == j
            rims = [jnp.where(hit, pieces[odd][q], rims[odd]) for odd in range(2)]
        rims.append(jnp.where(lane < LANES // 2, rims[0], rims[1]))
        for b, mask in enumerate(masks):
            at = slice(b * height, (b + 1) * height)
            rim = rims[2 if b == count else b // (count // 2)]
            out_ref[j, at, :] = jnp.where(mask, rim, packed_ref[j, at, :])


def partner(value, stride):
    if 2 * stride == MINI:
        return pltpu.roll(value, stride, 0)
    date = lax.broadcasted_iota(jnp.int32, value.shape, 0)
    up = pltpu.roll(value, MINI - stride, 0)
    down = pltpu.roll(value, stride, 0)
    return jnp.where((date // stride) % 2 == 0, up, down)


def link_kernel(tap_ref, coef_ref, data_ref, out_ref):
    blocks = 2
    nb = 2 * out_ref.shape[2] // blocks // LANES
    height = 4 * blocks
    stride = (nb + 1) * height
    lane = lax.broadcasted_iota(jnp.int32, (MINI, LANES), 1)
    date = lax.broadcasted_iota(jnp.int32, (MINI, LANES), 0)
    place_of = jnp.zeros((MINI, LANES), jnp.int32)
    for place, member in enumerate(ORDER):
        place_of = jnp.where(date == member, place, place_of)
    even_lane = 2 * lane % LANES

    def load(row):
        arrived = data_ref[pl.ds(row, MINI, stride=stride), :]
        return jnp.take_along_axis(arrived, place_of, axis=0)

    def sums_of(e, h):
        sums = None
        for p in range(2):
            pieces = []
            for c in range(2):
                row = (c * blocks + e) * 2 + p
                tail = load(nb * height + row)
                for odd in range(2):
                    block = odd * (nb // 2) + h
                    if h + 1 < nb // 2:
                        there = load((block + 1) * height + row)
                    else:
                        there = pltpu.roll(tail, LANES // 2, 1) if odd else tail
                    pieces.append((load(block * height + row), there))
            cache = {}

            def at(c, l):
                m, odd = l // 2, l % 2
                if (c, l) not in cache:
                    here, there = pieces[2 * c + odd]
                    if m:
                        here = pltpu.roll(jnp.where(lane < m, there, here), LANES - m, 1)
                    cache[c, l] = here
                return cache[c, l]

            centre = [[at(c, REACH + odd) for c in range(2)] for odd in range(2)]
            acc = [
                [[tap_ref[0] * centre[odd][c] for c in range(2)] for _ in range(ROUNDS)] for odd in range(2)
            ]
            for k in range(1, REACH + 1):
                for odd in range(2):
                    plus = [at(c, REACH + odd + k) for c in range(2)]
                    minus = [tap_ref[k] * at(c, REACH + odd - k) for c in range(2)]
                    even = [plus[c] + minus[c] for c in range(2)]
                    diff = [plus[c] - minus[c] for c in range(2)]
                    for r in range(ROUNDS):
                        j = r * REACH + k - 1
                        cosine, sine = coef_ref[2 * j], coef_ref[2 * j + 1]
                        total = acc[odd][r]
                        total[0] = total[0] + (cosine * even[0] - sine * diff[1])
                        total[1] = total[1] + (cosine * even[1] + sine * diff[0])
            for odd in range(2):
                terms = []
                for r in range(ROUNDS):
                    y_re, y_im = acc[odd][r]
                    z_re, z_im = partner(y_re, 1 << r), partner(y_im, 1 << r)
                    terms.append(y_re * z_re + y_im * z_im)
                    terms.append(y_im * z_re - y_re * z_im)
                terms.append(centre[odd][0] * centre[odd][0] + centre[odd][1] * centre[odd][1])
                sums = terms if sums is None else [s + t for s, t in zip(sums, terms)]
        return sums

    def energy_of(re, im):
        return jnp.sum(re * re + im * im, axis=0, keepdims=True)

    def shrink(length):
        return 1.0 / jnp.maximum(length, 1.0)

    for g in range(blocks * nb // 2):
        field = [total * 0.25 for total in sums_of(g // (nb // 2), g % (nb // 2))]
        vec_re = field[-1] + (field[0] + field[2] + field[4])
        vec_im = field[1] + field[3] + field[5]
        energies = [energy_of(vec_re, vec_im)]
        for _ in range(1, ITERS):
            next_re = field[-1] * vec_re
            next_im = field[-1] * vec_im
            for r in range(ROUNDS):
                o_re, o_im = partner(vec_re, 1 << r), partner(vec_im, 1 << r)
                t_re, t_im = field[2 * r], field[2 * r + 1]
                next_re = next_re + (t_re * o_re - t_im * o_im)
                next_im = next_im + (t_re * o_im + t_im * o_re)
            vec_re, vec_im = next_re, next_im
            energies.append(energy_of(vec_re, vec_im))
        factor = 1.0
        for energy in energies:
            factor = factor * shrink(jnp.sqrt(energy) * factor)
        out_ref[0, :, pl.ds(g * LANES, LANES)] = vec_re * factor
        out_ref[1, :, pl.ds(g * LANES, LANES)] = vec_im * factor


def to_owners(linked, inverse, blocks):
    date_count = lax.axis_size("date")
    position = lax.axis_index("date")
    parts = date_count // MINI
    member = position % MINI
    cut = linked.reshape(2, MINI, blocks, parts, -1)
    own_blocks = lax.dynamic_slice_in_dim(jnp.argsort(inverse), member * parts, parts)
    outgoing = jnp.zeros((date_count, 2, MINI, blocks, cut.shape[-1]), jnp.float32)
    outgoing = outgoing.at[own_blocks].set(jnp.moveaxis(cut, 3, 0))
    arrived = lax.all_to_all(outgoing, "date", split_axis=0, concat_axis=0, tiled=True)
    source = inverse[position] // parts
    arrived = arrived.reshape((parts, MINI) + arrived.shape[1:])
    chosen = lax.dynamic_index_in_dim(arrived, source, axis=1, keepdims=False)
    return jnp.moveaxis(chosen, 1, 0).reshape(2, date_count, -1)


def shards(slc_tiles, coreg_shift, center_freq, filter_taps, owner_table):
    own_tile = slc_tiles[:, 0]
    _, rows, cols = own_tile.shape
    date_count = lax.axis_size("date")
    strips = lax.axis_size("strip")
    blocks = coreg_shift.shape[1]
    share = rows // blocks // MINI
    position = lax.axis_index("date")
    other_tile = lax.ppermute(own_tile, "strip", [(s, strips - 1 - s) for s in range(strips)])
    if date_count == MINI:
        slots, freq = owner_table, center_freq
    else:
        slots = jnp.arange(MINI, dtype=jnp.int32)
        freq = lax.dynamic_slice_in_dim(center_freq, position // MINI * MINI, MINI)
    tall = 2 * blocks * share
    height = tall * (cols // LANES + 1)
    tile = (MINI, LANES)
    coefs, taps, slot_marks, shift_marks, packed = pl.pallas_call(
        prep_kernel,
        out_shape=(
            jax.ShapeDtypeStruct((2 * ROUNDS * REACH,) + tile, jnp.float32),
            jax.ShapeDtypeStruct((REACH + 1,) + tile, jnp.float32),
            jax.ShapeDtypeStruct((MINI,) + tile, jnp.int32),
            jax.ShapeDtypeStruct((blocks + 1,) + tile, jnp.int32),
            jax.ShapeDtypeStruct((MINI, height, LANES), jnp.float32),
        ),
        in_specs=[hbm()] * 5,
        out_specs=(vmem(),) * 5,
        scratch_shapes=[
            pltpu.SMEM(freq.shape, jnp.float32),
            pltpu.SMEM(filter_taps.shape, jnp.float32),
            pltpu.SMEM(slots.shape, jnp.int32),
            pltpu.SMEM(coreg_shift.shape, jnp.int32),
            pltpu.VMEM(own_tile.shape, jnp.float32),
            pltpu.SemaphoreType.DMA((5,)),
        ],
        compiler_params=params(),
        name="prep",
    )(*(in_hbm(x) for x in (freq, filter_taps, slots, coreg_shift, own_tile)))
    packed = pl.pallas_call(
        rim_kernel,
        out_shape=jax.ShapeDtypeStruct(packed.shape, jnp.float32),
        in_specs=[vmem()] * 4,
        out_specs=vmem(),
        input_output_aliases={3: 0},
        compiler_params=params(),
        name="rim",
    )(slot_marks, shift_marks, other_tile, packed)
    stacks = [[g + member for member in ORDER] for g in range(0, date_count, MINI)]
    data = lax.all_to_all(
        packed, "date", split_axis=0, concat_axis=0, axis_index_groups=stacks, tiled=True
    )
    linked = pl.pallas_call(
        link_kernel,
        out_shape=jax.ShapeDtypeStruct((2, MINI, blocks * share // 2 * cols // 2), jnp.float32),
        in_specs=[vmem()] * 3,
        out_specs=vmem(),
        compiler_params=params(),
        name="link",
    )(taps, coefs, data.reshape(-1, LANES))
    if date_count == MINI:
        return linked
    date_ids = jnp.arange(date_count, dtype=jnp.int32)
    inverse = jnp.zeros((date_count,), jnp.int32).at[owner_table].set(date_ids)
    return to_owners(linked, inverse, blocks)


def solution(mesh):
    in_specs = (
        P(None, ("groups", "date"), None, "strip"),
        P(("groups", "date"), None),
        P("groups"),
        P(),
        P("groups"),
    )
    out_specs = P(None, "groups", ("date", "strip"))
    return jax.shard_map(shards, mesh=mesh, in_specs=in_specs, out_specs=out_specs, check_vma=False)
```

```python
import jax
import jax.numpy as jnp
from jax import lax
from jax.experimental import pallas as pl
from jax.experimental.pallas import tpu as pltpu
from jax.sharding import PartitionSpec as P

SMAX = 16
TAPS = 17
ROUNDS = 3
MINI = 8
ITERS = 3
LANES = 128
REACH = TAPS // 2
ORDER = (5, 7, 3, 4, 0, 6, 1, 2)
LANE_BITS = LANES.bit_length() - 1
VMEM_LIMIT = 16 * 1024 * 1024


def vmem():
    return pl.BlockSpec(memory_space=pltpu.VMEM)


def hbm():
    return pl.BlockSpec(memory_space=pltpu.HBM)


def in_hbm(value):
    return pltpu.with_memory_space_constraint(value, pltpu.HBM)


def params():
    return pltpu.CompilerParams(vmem_limit_bytes=VMEM_LIMIT)


def sources(shift, lane, cols):
    first = [LANES - REACH - SMAX + shift + 2 * lane + odd for odd in range(2)]
    piece = [lax.shift_right_logical(f, LANE_BITS) for f in first]
    index = [2 * h + piece[odd] for odd in range(2) for h in range(cols // LANES // 2)]
    return [f & (LANES - 1) for f in first], index


def tails(lines_of, shift_of, wanted, lane, cols, blocks, share):
    count = cols // LANES
    row = lax.broadcasted_iota(jnp.int32, lane.shape, 0) % share
    column = 2 * (lane % REACH) + lane // REACH % 2
    total = jnp.zeros(lane.shape, jnp.float32)
    for e in range(blocks):
        first = LANES - REACH - SMAX + shift_of(e) + column
        mine = count + lax.shift_right_logical(first, LANE_BITS) == wanted
        for c in range(2):
            taken = jnp.take_along_axis(lines_of(c, e), first & (LANES - 1), axis=1)
            here = lane // (2 * REACH) == (c * blocks + e) * share + row
            total = jnp.where(mine & here, taken, total)
    return sum(pltpu.roll(total, (lane.shape[0] - p) % lane.shape[0], 0) if p else total for p in range(share))


def prep_kernel(
    freq_hbm, tap_hbm, slot_hbm, shift_hbm, tile_hbm,
    coef_ref, tap_out, slot_out, shift_out, packed_ref,
    freq_ref, tap_ref, slot_ref, shift_ref, tile_ref, sems,
):
    copies = [
        pltpu.make_async_copy(source, target, sems.at[i])
        for i, (source, target) in enumerate(
            (
                (freq_hbm, freq_ref),
                (shift_hbm, shift_ref),
                (slot_hbm, slot_ref),
                (tap_hbm, tap_ref),
                (tile_hbm, tile_ref),
            )
        )
    ]
    for copy in copies:
        copy.start()
    date = lax.broadcasted_iota(jnp.int32, (MINI, LANES), 0)
    lane = lax.broadcasted_iota(jnp.int32, (MINI, LANES), 1)
    for copy in copies[:4]:
        copy.wait()
    slots = []
    for q in range(MINI):
        slot = jnp.int32(0)
        for place, member in enumerate(ORDER):
            slot = jnp.where(slot_ref[q] == member, place, slot)
        slots.append(slot)

    def freq_of(index):
        total = jnp.zeros((MINI, LANES), jnp.float32)
        for d in range(MINI):
            total = jnp.where(index == d, freq_ref[d], total)
        return total

    own = freq_of(date)
    rotation = jnp.zeros((MINI, LANES), jnp.float32)
    for r in range(ROUNDS):
        q = jnp.pi * (freq_of(jnp.bitwise_xor(date, 1 << r)) - own)
        rotation = jnp.where(lane // REACH == r, q, rotation)
    angle = rotation * (lane % REACH + 1).astype(jnp.float32)
    cosine, sine = jnp.cos(angle), jnp.sin(angle)
    taps = [jnp.full((MINI, LANES), tap_ref[t], jnp.float32) for t in range(TAPS)]
    for j in range(ROUNDS * REACH):
        tap = taps[REACH + 1 + j % REACH]
        coef_ref[2 * j] = tap * jnp.broadcast_to(cosine[:, j : j + 1], (MINI, LANES))
        coef_ref[2 * j + 1] = tap * jnp.broadcast_to(sine[:, j : j + 1], (MINI, LANES))
    tap_out[0] = taps[REACH]
    for k in range(1, REACH + 1):
        tap_out[k] = taps[REACH - k] / taps[REACH + k]
    for q in range(MINI):
        slot_out[q] = jnp.full((MINI, LANES), slots[q], jnp.int32)
    _, rows, cols = tile_ref.shape
    blocks = shift_ref.shape[1]
    block_rows = rows // blocks
    share = block_rows // MINI
    tall = 2 * blocks * share
    height = packed_ref.shape[0] // MINI
    row = lax.broadcasted_iota(jnp.int32, (MINI, LANES), 0)
    offsets = jnp.zeros((MINI, LANES), jnp.int32)
    for e in range(blocks):
        offsets = jnp.where(row // share % blocks == e, shift_ref[0, e] + SMAX, offsets)
        shift_out[e] = jnp.full((MINI, LANES), shift_ref[0, e] + SMAX, jnp.int32)
    shift_out[blocks] = offsets
    count = cols // LANES
    tall_lane = lax.broadcasted_iota(jnp.int32, (block_rows, LANES), 1)
    plans = [sources(shift_ref[0, e] + SMAX, tall_lane, cols) for e in range(blocks)]
    copies[4].wait()
    for e in range(blocks):
        lanes, index = plans[e]
        for c in range(2):
            lines = pl.ds(e * block_rows, block_rows)
            taken = [
                [
                    jnp.take_along_axis(tile_ref[c, lines, v * LANES : (v + 1) * LANES], lanes[odd], axis=1)
                    for v in range(count)
                ]
                for odd in range(2)
            ]
            for b in range(count):
                value = jnp.zeros((block_rows, LANES), jnp.float32)
                low = b % (count // 2) * 2
                for v in range(max(low, 1), min(low + 3, count) + 1):
                    value = jnp.where(index[b] == v, taken[b // (count // 2)][v - 1], value)
                at = b * tall + (c * blocks + e) * share
                for q in range(MINI):
                    packed_ref[pl.ds(slots[q] * height + at, share), :] = value[q * share : (q + 1) * share]
    rest = tails(
        lambda c, e: tile_ref[c, e * block_rows : (e + 1) * block_rows, cols - LANES : cols],
        lambda e: shift_ref[0, e] + SMAX,
        count, tall_lane, cols, blocks, share,
    )
    for q in range(MINI):
        packed_ref[pl.ds(slots[q] * height + count * tall, 1), :] = rest[q * share : q * share + 1]


def rim_kernel(slot_ref, shift_ref, other_ref, packed_ref, out_ref):
    _, rows, cols = other_ref.shape
    blocks = shift_ref.shape[0] - 1
    block_rows = rows // blocks
    share = block_rows // MINI
    tall = 2 * blocks * share
    height = packed_ref.shape[0] // MINI
    count = cols // LANES
    first = lax.axis_index("strip") == 0
    lane = lax.broadcasted_iota(jnp.int32, (MINI, LANES), 1)
    tall_lane = lax.broadcasted_iota(jnp.int32, (block_rows, LANES), 1)
    rim_of, shift_of, moved = {}, [], []
    for e in range(blocks):
        shift_of.append(jnp.concatenate([shift_ref[e]] * (block_rows // MINI), axis=0))
    for c in range(2):
        for e in range(blocks):
            lines = pl.ds(e * block_rows, block_rows)
            rim = jnp.where(first, other_ref[c, lines, 0:LANES], other_ref[c, lines, cols - LANES : cols])
            lanes, _ = sources(shift_of[e], tall_lane, cols)
            moved.append([jnp.take_along_axis(rim, lanes[odd], axis=1) for odd in range(2)])
            rim_of[c, e] = rim
    pieces = [
        [jnp.concatenate([m[odd][q * share : (q + 1) * share] for m in moved], axis=0) for q in range(MINI)]
        for odd in range(2)
    ]
    _, index = sources(shift_ref[blocks], lane, cols)
    wanted = jnp.where(first, count + 1, 0)
    masks = [piece == wanted for piece in index]
    rest = tails(
        lambda c, e: rim_of[c, e], lambda e: shift_of[e], wanted, tall_lane, cols, blocks, share
    )
    slot = lax.broadcasted_iota(jnp.int32, (MINI, LANES), 0)
    ends = jnp.zeros((MINI, LANES), jnp.float32)
    for q in range(MINI):
        ends = jnp.where(slot == slot_ref[q], rest[q * share : q * share + 1], ends)
    for j in range(MINI):
        rims = [pieces[odd][0] for odd in range(2)]
        for q in range(1, MINI):
            hit = slot_ref[q] == j
            rims = [jnp.where(hit, pieces[odd][q], rims[odd]) for odd in range(2)]
        for b, mask in enumerate(masks):
            at = slice(j * height + b * tall, j * height + (b + 1) * tall)
            out_ref[at, :] = jnp.where(mask, rims[b // (count // 2)], packed_ref[at, :])
        at = slice((j + 1) * height - 1, (j + 1) * height)
        out_ref[at, :] = packed_ref[at, :] + ends[j : j + 1]


def partner(value, stride):
    if 2 * stride == MINI:
        return pltpu.roll(value, stride, 0)
    date = lax.broadcasted_iota(jnp.int32, value.shape, 0)
    up = pltpu.roll(value, MINI - stride, 0)
    down = pltpu.roll(value, stride, 0)
    return jnp.where((date // stride) % 2 == 0, up, down)


def link_kernel(tap_ref, coef_ref, data_ref, out_ref):
    blocks = 2
    nb = 2 * out_ref.shape[2] // blocks // LANES
    tall = 4 * blocks
    stride = nb * tall + 1
    lane = lax.broadcasted_iota(jnp.int32, (MINI, LANES), 1)
    date = lax.broadcasted_iota(jnp.int32, (MINI, LANES), 0)
    place_of = jnp.zeros((MINI, LANES), jnp.int32)
    for place, member in enumerate(ORDER):
        place_of = jnp.where(date == member, place, place_of)
    even_lane = 2 * lane % LANES

    def load(row):
        arrived = data_ref[pl.ds(row, MINI, stride=stride), :]
        return jnp.take_along_axis(arrived, place_of, axis=0)

    def sums_of(e, h):
        sums = None
        ends = load(nb * tall)
        for p in range(2):
            pieces = []
            for c in range(2):
                row = (c * blocks + e) * 2 + p
                for odd in range(2):
                    block = odd * (nb // 2) + h
                    if h + 1 < nb // 2:
                        there = load((block + 1) * tall + row)
                    else:
                        there = pltpu.roll(ends, (LANES - (2 * row + odd) * REACH) % LANES, 1)
                    pieces.append((load(block * tall + row), there))
            cache = {}

            def at(c, l):
                m, odd = l // 2, l % 2
                if (c, l) not in cache:
                    here, there = pieces[2 * c + odd]
                    if m:
                        here = pltpu.roll(jnp.where(lane < m, there, here), LANES - m, 1)
                    cache[c, l] = here
                return cache[c, l]

            centre = [[at(c, REACH + odd) for c in range(2)] for odd in range(2)]
            acc = [
                [[tap_ref[0] * centre[odd][c] for c in range(2)] for _ in range(ROUNDS)] for odd in range(2)
            ]
            for k in range(1, REACH + 1):
                for odd in range(2):
                    plus = [at(c, REACH + odd + k) for c in range(2)]
                    minus = [tap_ref[k] * at(c, REACH + odd - k) for c in range(2)]
                    even = [plus[c] + minus[c] for c in range(2)]
                    diff = [plus[c] - minus[c] for c in range(2)]
                    for r in range(ROUNDS):
                        j = r * REACH + k - 1
                        cosine, sine = coef_ref[2 * j], coef_ref[2 * j + 1]
                        total = acc[odd][r]
                        total[0] = total[0] + (cosine * even[0] - sine * diff[1])
                        total[1] = total[1] + (cosine * even[1] + sine * diff[0])
            for odd in range(2):
                terms = []
                for r in range(ROUNDS):
                    y_re, y_im = acc[odd][r]
                    z_re, z_im = partner(y_re, 1 << r), partner(y_im, 1 << r)
                    terms.append(y_re * z_re + y_im * z_im)
                    terms.append(y_im * z_re - y_re * z_im)
                terms.append(centre[odd][0] * centre[odd][0] + centre[odd][1] * centre[odd][1])
                sums = terms if sums is None else [s + t for s, t in zip(sums, terms)]
        return sums

    def energy_of(re, im):
        return jnp.sum(re * re + im * im, axis=0, keepdims=True)

    def shrink(length):
        return 1.0 / jnp.maximum(length, 1.0)

    for g in range(blocks * nb // 2):
        field = [total * 0.25 for total in sums_of(g // (nb // 2), g % (nb // 2))]
        vec_re = field[-1] + (field[0] + field[2] + field[4])
        vec_im = field[1] + field[3] + field[5]
        energies = [energy_of(vec_re, vec_im)]
        for _ in range(1, ITERS):
            next_re = field[-1] * vec_re
            next_im = field[-1] * vec_im
            for r in range(ROUNDS):
                o_re, o_im = partner(vec_re, 1 << r), partner(vec_im, 1 << r)
                t_re, t_im = field[2 * r], field[2 * r + 1]
                next_re = next_re + (t_re * o_re - t_im * o_im)
                next_im = next_im + (t_re * o_im + t_im * o_re)
            vec_re, vec_im = next_re, next_im
            energies.append(energy_of(vec_re, vec_im))
        factor = 1.0
        for energy in energies:
            factor = factor * shrink(jnp.sqrt(energy) * factor)
        out_ref[0, :, pl.ds(g * LANES, LANES)] = vec_re * factor
        out_ref[1, :, pl.ds(g * LANES, LANES)] = vec_im * factor


def to_owners(linked, inverse, blocks):
    date_count = lax.axis_size("date")
    position = lax.axis_index("date")
    parts = date_count // MINI
    member = position % MINI
    cut = linked.reshape(2, MINI, blocks, parts, -1)
    own_blocks = lax.dynamic_slice_in_dim(jnp.argsort(inverse), member * parts, parts)
    outgoing = jnp.zeros((date_count, 2, MINI, blocks, cut.shape[-1]), jnp.float32)
    outgoing = outgoing.at[own_blocks].set(jnp.moveaxis(cut, 3, 0))
    arrived = lax.all_to_all(outgoing, "date", split_axis=0, concat_axis=0, tiled=True)
    source = inverse[position] // parts
    arrived = arrived.reshape((parts, MINI) + arrived.shape[1:])
    chosen = lax.dynamic_index_in_dim(arrived, source, axis=1, keepdims=False)
    return jnp.moveaxis(chosen, 1, 0).reshape(2, date_count, -1)


def shards(slc_tiles, coreg_shift, center_freq, filter_taps, owner_table):
    own_tile = slc_tiles[:, 0]
    _, rows, cols = own_tile.shape
    date_count = lax.axis_size("date")
    strips = lax.axis_size("strip")
    blocks = coreg_shift.shape[1]
    share = rows // blocks // MINI
    position = lax.axis_index("date")
    other_tile = lax.ppermute(own_tile, "strip", [(s, strips - 1 - s) for s in range(strips)])
    if date_count == MINI:
        slots, freq = owner_table, center_freq
    else:
        slots = jnp.arange(MINI, dtype=jnp.int32)
        freq = lax.dynamic_slice_in_dim(center_freq, position // MINI * MINI, MINI)
    tall = 2 * blocks * share
    height = tall * (cols // LANES) + 1
    tile = (MINI, LANES)
    coefs, taps, slot_marks, shift_marks, packed = pl.pallas_call(
        prep_kernel,
        out_shape=(
            jax.ShapeDtypeStruct((2 * ROUNDS * REACH,) + tile, jnp.float32),
            jax.ShapeDtypeStruct((REACH + 1,) + tile, jnp.float32),
            jax.ShapeDtypeStruct((MINI,) + tile, jnp.int32),
            jax.ShapeDtypeStruct((blocks + 1,) + tile, jnp.int32),
            jax.ShapeDtypeStruct((MINI * height, LANES), jnp.float32),
        ),
        in_specs=[hbm()] * 5,
        out_specs=(vmem(),) * 5,
        scratch_shapes=[
            pltpu.SMEM(freq.shape, jnp.float32),
            pltpu.SMEM(filter_taps.shape, jnp.float32),
            pltpu.SMEM(slots.shape, jnp.int32),
            pltpu.SMEM(coreg_shift.shape, jnp.int32),
            pltpu.VMEM(own_tile.shape, jnp.float32),
            pltpu.SemaphoreType.DMA((5,)),
        ],
        compiler_params=params(),
        name="prep",
    )(*(in_hbm(x) for x in (freq, filter_taps, slots, coreg_shift, own_tile)))
    packed = pl.pallas_call(
        rim_kernel,
        out_shape=jax.ShapeDtypeStruct(packed.shape, jnp.float32),
        in_specs=[vmem()] * 4,
        out_specs=vmem(),
        input_output_aliases={3: 0},
        compiler_params=params(),
        name="rim",
    )(slot_marks, shift_marks, other_tile, packed)
    stacks = [[g + member for member in ORDER] for g in range(0, date_count, MINI)]
    data = lax.all_to_all(
        packed.reshape(MINI, 1, height * LANES), "date", split_axis=0, concat_axis=0, axis_index_groups=stacks, tiled=True
    )
    linked = pl.pallas_call(
        link_kernel,
        out_shape=jax.ShapeDtypeStruct((2, MINI, blocks * share // 2 * cols // 2), jnp.float32),
        in_specs=[vmem()] * 3,
        out_specs=vmem(),
        compiler_params=params(),
        name="link",
    )(taps, coefs, data.reshape(-1, LANES))
    if date_count == MINI:
        return linked
    date_ids = jnp.arange(date_count, dtype=jnp.int32)
    inverse = jnp.zeros((date_count,), jnp.int32).at[owner_table].set(date_ids)
    return to_owners(linked, inverse, blocks)


def solution(mesh):
    in_specs = (
        P(None, ("groups", "date"), None, "strip"),
        P(("groups", "date"), None),
        P("groups"),
        P(),
        P("groups"),
    )
    out_specs = P(None, "groups", ("date", "strip"))
    return jax.shard_map(shards, mesh=mesh, in_specs=in_specs, out_specs=out_specs, check_vma=False)
```

```python
import jax
import jax.numpy as jnp
from jax import lax
from jax.experimental import pallas as pl
from jax.experimental.pallas import tpu as pltpu
from jax.sharding import PartitionSpec as P

SMAX = 16
TAPS = 17
ROUNDS = 3
MINI = 8
ITERS = 3
LANES = 128
REACH = TAPS // 2
ORDER = (5, 7, 3, 4, 0, 6, 1, 2)
LANE_BITS = LANES.bit_length() - 1
VMEM_LIMIT = 16 * 1024 * 1024


def vmem():
    return pl.BlockSpec(memory_space=pltpu.VMEM)


def hbm():
    return pl.BlockSpec(memory_space=pltpu.HBM)


def in_hbm(value):
    return pltpu.with_memory_space_constraint(value, pltpu.HBM)


def params():
    return pltpu.CompilerParams(vmem_limit_bytes=VMEM_LIMIT)


def table(entries, shape):
    row = lax.broadcasted_iota(jnp.int32, shape, 0)
    result = jnp.full(shape, entries[0], jnp.int32)
    for i, entry in enumerate(entries[1:], 1):
        result = jnp.where(row == i, entry, result)
    return result


def sources(shift, lane, cols):
    first = [LANES - REACH - SMAX + shift + 2 * lane + odd for odd in range(2)]
    piece = [lax.shift_right_logical(f, LANE_BITS) for f in first]
    index = [2 * h + piece[odd] for odd in range(2) for h in range(cols // LANES // 2)]
    return [f & (LANES - 1) for f in first], index


def tails(lines_of, shift_of, wanted, lane, cols, blocks, share):
    count = cols // LANES
    row = lax.broadcasted_iota(jnp.int32, lane.shape, 0) % share
    column = 2 * (lane % REACH) + lane // REACH % 2
    total = jnp.zeros(lane.shape, jnp.float32)
    for e in range(blocks):
        first = LANES - REACH - SMAX + shift_of(e) + column
        mine = count + lax.shift_right_logical(first, LANE_BITS) == wanted
        for c in range(2):
            taken = jnp.take_along_axis(lines_of(c, e), first & (LANES - 1), axis=1)
            here = lane // (2 * REACH) == (c * blocks + e) * share + row
            total = jnp.where(mine & here, taken, total)
    return sum(pltpu.roll(total, (lane.shape[0] - p) % lane.shape[0], 0) if p else total for p in range(share))


def prep_kernel(
    freq_hbm, tap_hbm, slot_hbm, shift_hbm, tile_hbm,
    coef_ref, tap_out, slot_out, shift_out, packed_ref,
    freq_ref, tap_ref, slot_ref, shift_ref, tile_ref, sems,
):
    copies = [
        pltpu.make_async_copy(source, target, sems.at[i])
        for i, (source, target) in enumerate(
            (
                (freq_hbm, freq_ref),
                (shift_hbm, shift_ref),
                (slot_hbm, slot_ref),
                (tap_hbm, tap_ref),
                (tile_hbm, tile_ref),
            )
        )
    ]
    for copy in copies:
        copy.start()
    date = table(ORDER, (MINI, LANES))
    lane = lax.broadcasted_iota(jnp.int32, (MINI, LANES), 1)
    for copy in copies[:4]:
        copy.wait()
    slots = []
    for q in range(MINI):
        slot = jnp.int32(0)
        for place, member in enumerate(ORDER):
            slot = jnp.where(slot_ref[q] == member, place, slot)
        slots.append(slot)

    def freq_of(index):
        total = jnp.zeros((MINI, LANES), jnp.float32)
        for d in range(MINI):
            total = jnp.where(index == d, freq_ref[d], total)
        return total

    own = freq_of(date)
    rotation = jnp.zeros((MINI, LANES), jnp.float32)
    for r in range(ROUNDS):
        q = jnp.pi * (freq_of(jnp.bitwise_xor(date, 1 << r)) - own)
        rotation = jnp.where(lane // REACH == r, q, rotation)
    angle = rotation * (lane % REACH + 1).astype(jnp.float32)
    cosine, sine = jnp.cos(angle), jnp.sin(angle)
    taps = [jnp.full((MINI, LANES), tap_ref[t], jnp.float32) for t in range(TAPS)]
    for j in range(ROUNDS * REACH):
        tap = 0.5 * taps[REACH + 1 + j % REACH]
        coef_ref[2 * j] = tap * jnp.broadcast_to(cosine[:, j : j + 1], (MINI, LANES))
        coef_ref[2 * j + 1] = tap * jnp.broadcast_to(sine[:, j : j + 1], (MINI, LANES))
    tap_out[0] = 0.5 * taps[REACH]
    for k in range(1, REACH + 1):
        tap_out[k] = taps[REACH - k] / taps[REACH + k]
    for q in range(MINI):
        slot_out[q] = jnp.full((MINI, LANES), slots[q], jnp.int32)
    _, rows, cols = tile_ref.shape
    blocks = shift_ref.shape[1]
    block_rows = rows // blocks
    share = block_rows // MINI
    tall = 2 * blocks * share
    height = packed_ref.shape[0] // MINI
    row = lax.broadcasted_iota(jnp.int32, (MINI, LANES), 0)
    offsets = jnp.zeros((MINI, LANES), jnp.int32)
    for e in range(blocks):
        offsets = jnp.where(row // share % blocks == e, shift_ref[0, e] + SMAX, offsets)
        shift_out[e] = jnp.full((MINI, LANES), shift_ref[0, e] + SMAX, jnp.int32)
    shift_out[blocks] = offsets
    count = cols // LANES
    tall_lane = lax.broadcasted_iota(jnp.int32, (block_rows, LANES), 1)
    plans = [sources(shift_ref[0, e] + SMAX, tall_lane, cols) for e in range(blocks)]
    copies[4].wait()
    for e in range(blocks):
        lanes, index = plans[e]
        for c in range(2):
            lines = pl.ds(e * block_rows, block_rows)
            taken = [
                [
                    jnp.take_along_axis(tile_ref[c, lines, v * LANES : (v + 1) * LANES], lanes[odd], axis=1)
                    for v in range(count)
                ]
                for odd in range(2)
            ]
            for b in range(count):
                value = jnp.zeros((block_rows, LANES), jnp.float32)
                low = b % (count // 2) * 2
                for v in range(max(low, 1), min(low + 3, count) + 1):
                    value = jnp.where(index[b] == v, taken[b // (count // 2)][v - 1], value)
                at = b * tall + (c * blocks + e) * share
                for q in range(MINI):
                    packed_ref[pl.ds(slots[q] * height + at, share), :] = value[q * share : (q + 1) * share]
    rest = tails(
        lambda c, e: tile_ref[c, e * block_rows : (e + 1) * block_rows, cols - LANES : cols],
        lambda e: shift_ref[0, e] + SMAX,
        count, tall_lane, cols, blocks, share,
    )
    for q in range(MINI):
        packed_ref[pl.ds(slots[q] * height + count * tall, 1), :] = rest[q * share : q * share + 1]


def rim_kernel(slot_ref, shift_ref, other_ref, packed_ref, out_ref):
    _, rows, cols = other_ref.shape
    blocks = shift_ref.shape[0] - 1
    block_rows = rows // blocks
    share = block_rows // MINI
    tall = 2 * blocks * share
    height = packed_ref.shape[0] // MINI
    count = cols // LANES
    first = lax.axis_index("strip") == 0
    lane = lax.broadcasted_iota(jnp.int32, (MINI, LANES), 1)
    tall_lane = lax.broadcasted_iota(jnp.int32, (block_rows, LANES), 1)
    rim_of, shift_of, moved = {}, [], []
    for e in range(blocks):
        shift_of.append(jnp.concatenate([shift_ref[e]] * (block_rows // MINI), axis=0))
    for c in range(2):
        for e in range(blocks):
            lines = pl.ds(e * block_rows, block_rows)
            rim = jnp.where(first, other_ref[c, lines, 0:LANES], other_ref[c, lines, cols - LANES : cols])
            lanes, _ = sources(shift_of[e], tall_lane, cols)
            moved.append([jnp.take_along_axis(rim, lanes[odd], axis=1) for odd in range(2)])
            rim_of[c, e] = rim
    pieces = [
        [jnp.concatenate([m[odd][q * share : (q + 1) * share] for m in moved], axis=0) for q in range(MINI)]
        for odd in range(2)
    ]
    _, index = sources(shift_ref[blocks], lane, cols)
    wanted = jnp.where(first, count + 1, 0)
    masks = [piece == wanted for piece in index]
    rest = tails(
        lambda c, e: rim_of[c, e], lambda e: shift_of[e], wanted, tall_lane, cols, blocks, share
    )
    slot = lax.broadcasted_iota(jnp.int32, (MINI, LANES), 0)
    ends = jnp.zeros((MINI, LANES), jnp.float32)
    for q in range(MINI):
        ends = jnp.where(slot == slot_ref[q], rest[q * share : q * share + 1], ends)
    for j in range(MINI):
        rims = [pieces[odd][0] for odd in range(2)]
        for q in range(1, MINI):
            hit = slot_ref[q] == j
            rims = [jnp.where(hit, pieces[odd][q], rims[odd]) for odd in range(2)]
        for b, mask in enumerate(masks):
            at = slice(j * height + b * tall, j * height + (b + 1) * tall)
            out_ref[at, :] = jnp.where(mask, rims[b // (count // 2)], packed_ref[at, :])
        at = slice((j + 1) * height - 1, (j + 1) * height)
        out_ref[at, :] = packed_ref[at, :] + ends[j : j + 1]


def partner(value, stride):
    places = [ORDER.index(member ^ stride) for member in ORDER]
    return jnp.take_along_axis(value, table(places, value.shape), axis=0)


def link_kernel(tap_ref, coef_ref, data_ref, out_ref):
    blocks = 2
    nb = 2 * out_ref.shape[2] // blocks // LANES
    tall = 4 * blocks
    stride = nb * tall + 1
    lane = lax.broadcasted_iota(jnp.int32, (MINI, LANES), 1)
    by_date = table([ORDER.index(d) for d in range(MINI)], (MINI, LANES))

    def load(row):
        return data_ref[pl.ds(row, MINI, stride=stride), :]

    def sums_of(e, h):
        sums = None
        ends = load(nb * tall)
        for p in range(2):
            pieces = []
            for c in range(2):
                row = (c * blocks + e) * 2 + p
                for odd in range(2):
                    block = odd * (nb // 2) + h
                    if h + 1 < nb // 2:
                        there = load((block + 1) * tall + row)
                    else:
                        there = pltpu.roll(ends, (LANES - (2 * row + odd) * REACH) % LANES, 1)
                    pieces.append((load(block * tall + row), there))
            cache = {}

            def at(c, l):
                m, odd = l // 2, l % 2
                if (c, l) not in cache:
                    here, there = pieces[2 * c + odd]
                    if m:
                        here = pltpu.roll(jnp.where(lane < m, there, here), LANES - m, 1)
                    cache[c, l] = here
                return cache[c, l]

            centre = [[at(c, REACH + odd) for c in range(2)] for odd in range(2)]
            acc = [
                [[tap_ref[0] * centre[odd][c] for c in range(2)] for _ in range(ROUNDS)] for odd in range(2)
            ]
            for k in range(1, REACH + 1):
                for odd in range(2):
                    plus = [at(c, REACH + odd + k) for c in range(2)]
                    minus = [tap_ref[k] * at(c, REACH + odd - k) for c in range(2)]
                    even = [plus[c] + minus[c] for c in range(2)]
                    diff = [plus[c] - minus[c] for c in range(2)]
                    for r in range(ROUNDS):
                        j = r * REACH + k - 1
                        cosine, sine = coef_ref[2 * j], coef_ref[2 * j + 1]
                        total = acc[odd][r]
                        total[0] = total[0] + (cosine * even[0] - sine * diff[1])
                        total[1] = total[1] + (cosine * even[1] + sine * diff[0])
            for odd in range(2):
                terms = []
                for r in range(ROUNDS):
                    y_re, y_im = acc[odd][r]
                    z_re, z_im = partner(y_re, 1 << r), partner(y_im, 1 << r)
                    terms.append(y_re * z_re + y_im * z_im)
                    terms.append(y_im * z_re - y_re * z_im)
                terms.append(centre[odd][0] * centre[odd][0] + centre[odd][1] * centre[odd][1])
                sums = terms if sums is None else [s + t for s, t in zip(sums, terms)]
        return sums

    def energy_of(re, im):
        return jnp.sum(re * re + im * im, axis=0, keepdims=True)

    def shrink(length):
        return 1.0 / jnp.maximum(length, 1.0)

    for g in range(blocks * nb // 2):
        field = sums_of(g // (nb // 2), g % (nb // 2))
        field[-1] = field[-1] * 0.25
        vec_re = field[-1] + (field[0] + field[2] + field[4])
        vec_im = field[1] + field[3] + field[5]
        energies = [energy_of(vec_re, vec_im)]
        for _ in range(1, ITERS):
            next_re = field[-1] * vec_re
            next_im = field[-1] * vec_im
            for r in range(ROUNDS):
                o_re, o_im = partner(vec_re, 1 << r), partner(vec_im, 1 << r)
                t_re, t_im = field[2 * r], field[2 * r + 1]
                next_re = next_re + (t_re * o_re - t_im * o_im)
                next_im = next_im + (t_re * o_im + t_im * o_re)
            vec_re, vec_im = next_re, next_im
            energies.append(energy_of(vec_re, vec_im))
        factor = 1.0
        for energy in energies:
            factor = factor * shrink(jnp.sqrt(energy) * factor)
        for c, vec in enumerate((vec_re, vec_im)):
            out_ref[c, :, pl.ds(g * LANES, LANES)] = jnp.take_along_axis(vec * factor, by_date, axis=0)


def to_owners(linked, inverse, blocks):
    date_count = lax.axis_size("date")
    position = lax.axis_index("date")
    parts = date_count // MINI
    member = position % MINI
    cut = linked.reshape(2, MINI, blocks, parts, -1)
    own_blocks = lax.dynamic_slice_in_dim(jnp.argsort(inverse), member * parts, parts)
    outgoing = jnp.zeros((date_count, 2, MINI, blocks, cut.shape[-1]), jnp.float32)
    outgoing = outgoing.at[own_blocks].set(jnp.moveaxis(cut, 3, 0))
    arrived = lax.all_to_all(outgoing, "date", split_axis=0, concat_axis=0, tiled=True)
    source = inverse[position] // parts
    arrived = arrived.reshape((parts, MINI) + arrived.shape[1:])
    chosen = lax.dynamic_index_in_dim(arrived, source, axis=1, keepdims=False)
    return jnp.moveaxis(chosen, 1, 0).reshape(2, date_count, -1)


def shards(slc_tiles, coreg_shift, center_freq, filter_taps, owner_table):
    own_tile = slc_tiles[:, 0]
    _, rows, cols = own_tile.shape
    date_count = lax.axis_size("date")
    strips = lax.axis_size("strip")
    blocks = coreg_shift.shape[1]
    share = rows // blocks // MINI
    position = lax.axis_index("date")
    other_tile = lax.ppermute(own_tile, "strip", [(s, strips - 1 - s) for s in range(strips)])
    if date_count == MINI:
        slots, freq = owner_table, center_freq
    else:
        slots = jnp.arange(MINI, dtype=jnp.int32)
        freq = lax.dynamic_slice_in_dim(center_freq, position // MINI * MINI, MINI)
    tall = 2 * blocks * share
    height = tall * (cols // LANES) + 1
    tile = (MINI, LANES)
    coefs, taps, slot_marks, shift_marks, packed = pl.pallas_call(
        prep_kernel,
        out_shape=(
            jax.ShapeDtypeStruct((2 * ROUNDS * REACH,) + tile, jnp.float32),
            jax.ShapeDtypeStruct((REACH + 1,) + tile, jnp.float32),
            jax.ShapeDtypeStruct((MINI,) + tile, jnp.int32),
            jax.ShapeDtypeStruct((blocks + 1,) + tile, jnp.int32),
            jax.ShapeDtypeStruct((MINI * height, LANES), jnp.float32),
        ),
        in_specs=[hbm()] * 5,
        out_specs=(vmem(),) * 5,
        scratch_shapes=[
            pltpu.SMEM(freq.shape, jnp.float32),
            pltpu.SMEM(filter_taps.shape, jnp.float32),
            pltpu.SMEM(slots.shape, jnp.int32),
            pltpu.SMEM(coreg_shift.shape, jnp.int32),
            pltpu.VMEM(own_tile.shape, jnp.float32),
            pltpu.SemaphoreType.DMA((5,)),
        ],
        compiler_params=params(),
        name="prep",
    )(*(in_hbm(x) for x in (freq, filter_taps, slots, coreg_shift, own_tile)))
    packed = pl.pallas_call(
        rim_kernel,
        out_shape=jax.ShapeDtypeStruct(packed.shape, jnp.float32),
        in_specs=[vmem()] * 4,
        out_specs=vmem(),
        input_output_aliases={3: 0},
        compiler_params=params(),
        name="rim",
    )(slot_marks, shift_marks, other_tile, packed)
    stacks = [[g + member for member in ORDER] for g in range(0, date_count, MINI)]
    data = lax.all_to_all(
        packed.reshape(MINI, 1, height * LANES), "date", split_axis=0, concat_axis=0, axis_index_groups=stacks, tiled=True
    )
    linked = pl.pallas_call(
        link_kernel,
        out_shape=jax.ShapeDtypeStruct((2, MINI, blocks * share // 2 * cols // 2), jnp.float32),
        in_specs=[vmem()] * 3,
        out_specs=vmem(),
        compiler_params=params(),
        name="link",
    )(taps, coefs, data.reshape(-1, LANES))
    if date_count == MINI:
        return linked
    date_ids = jnp.arange(date_count, dtype=jnp.int32)
    inverse = jnp.zeros((date_count,), jnp.int32).at[owner_table].set(date_ids)
    return to_owners(linked, inverse, blocks)


def solution(mesh):
    in_specs = (
        P(None, ("groups", "date"), None, "strip"),
        P(("groups", "date"), None),
        P("groups"),
        P(),
        P("groups"),
    )
    out_specs = P(None, "groups", ("date", "strip"))
    return jax.shard_map(shards, mesh=mesh, in_specs=in_specs, out_specs=out_specs, check_vma=False)
```

```python
import jax
import jax.numpy as jnp
from jax import lax
from jax.experimental import pallas as pl
from jax.experimental.pallas import tpu as pltpu
from jax.sharding import PartitionSpec as P

SMAX = 16
TAPS = 17
ROUNDS = 3
MINI = 8
ITERS = 3
LANES = 128
REACH = TAPS // 2
ORDER = (5, 6, 3, 2, 0, 7, 4, 1)
LANE_BITS = LANES.bit_length() - 1
VMEM_LIMIT = 16 * 1024 * 1024


def vmem():
    return pl.BlockSpec(memory_space=pltpu.VMEM)


def hbm():
    return pl.BlockSpec(memory_space=pltpu.HBM)


def in_hbm(value):
    return pltpu.with_memory_space_constraint(value, pltpu.HBM)


def params():
    return pltpu.CompilerParams(vmem_limit_bytes=VMEM_LIMIT)


def table(entries, shape):
    row = lax.broadcasted_iota(jnp.int32, shape, 0)
    result = jnp.full(shape, entries[0], jnp.int32)
    for i, entry in enumerate(entries[1:], 1):
        result = jnp.where(row == i, entry, result)
    return result


def sources(shift, lane, cols):
    first = [LANES - REACH - SMAX + shift + 2 * lane + odd for odd in range(2)]
    piece = [lax.shift_right_logical(f, LANE_BITS) for f in first]
    index = [2 * h + piece[odd] for odd in range(2) for h in range(cols // LANES // 2)]
    return [f & (LANES - 1) for f in first], index


def tails(lines_of, shift_of, wanted, lane, cols, blocks, share):
    count = cols // LANES
    row = lax.broadcasted_iota(jnp.int32, lane.shape, 0) % share
    column = 2 * (lane % REACH) + lane // REACH % 2
    total = jnp.zeros(lane.shape, jnp.float32)
    for e in range(blocks):
        first = LANES - REACH - SMAX + shift_of(e) + column
        mine = count + lax.shift_right_logical(first, LANE_BITS) == wanted
        for c in range(2):
            taken = jnp.take_along_axis(lines_of(c, e), first & (LANES - 1), axis=1)
            here = lane // (2 * REACH) == (c * blocks + e) * share + row
            total = jnp.where(mine & here, taken, total)
    return sum(pltpu.roll(total, (lane.shape[0] - p) % lane.shape[0], 0) if p else total for p in range(share))


def prep_kernel(
    freq_hbm, tap_hbm, slot_hbm, shift_hbm, tile_hbm,
    coef_ref, tap_out, slot_out, shift_out, packed_ref,
    freq_ref, tap_ref, slot_ref, shift_ref, tile_ref, sems,
):
    copies = [
        pltpu.make_async_copy(source, target, sems.at[i])
        for i, (source, target) in enumerate(
            (
                (freq_hbm, freq_ref),
                (shift_hbm, shift_ref),
                (slot_hbm, slot_ref),
                (tap_hbm, tap_ref),
                (tile_hbm, tile_ref),
            )
        )
    ]
    for copy in copies:
        copy.start()
    date = table(ORDER, (MINI, LANES))
    lane = lax.broadcasted_iota(jnp.int32, (MINI, LANES), 1)
    for copy in copies[:4]:
        copy.wait()
    slots = []
    for q in range(MINI):
        slot = jnp.int32(0)
        for place, member in enumerate(ORDER):
            slot = jnp.where(slot_ref[q] == member, place, slot)
        slots.append(slot)

    def freq_of(index):
        total = jnp.zeros((MINI, LANES), jnp.float32)
        for d in range(MINI):
            total = jnp.where(index == d, freq_ref[d], total)
        return total

    own = freq_of(date)
    rotation = jnp.zeros((MINI, LANES), jnp.float32)
    for r in range(ROUNDS):
        q = jnp.pi * (freq_of(jnp.bitwise_xor(date, 1 << r)) - own)
        rotation = jnp.where(lane // REACH == r, q, rotation)
    angle = rotation * (lane % REACH + 1).astype(jnp.float32)
    cosine, sine = jnp.cos(angle), jnp.sin(angle)
    taps = [jnp.full((MINI, LANES), tap_ref[t], jnp.float32) for t in range(TAPS)]
    for j in range(ROUNDS * REACH):
        tap = 0.5 * taps[REACH + 1 + j % REACH]
        coef_ref[2 * j] = tap * jnp.broadcast_to(cosine[:, j : j + 1], (MINI, LANES))
        coef_ref[2 * j + 1] = tap * jnp.broadcast_to(sine[:, j : j + 1], (MINI, LANES))
    tap_out[0] = 0.5 * taps[REACH]
    for k in range(1, REACH + 1):
        tap_out[k] = taps[REACH - k] / taps[REACH + k]
    for q in range(MINI):
        slot_out[q] = jnp.full((MINI, LANES), slots[q], jnp.int32)
    _, rows, cols = tile_ref.shape
    blocks = shift_ref.shape[1]
    block_rows = rows // blocks
    share = block_rows // MINI
    tall = 2 * blocks * share
    height = packed_ref.shape[0] // MINI
    row = lax.broadcasted_iota(jnp.int32, (MINI, LANES), 0)
    offsets = jnp.zeros((MINI, LANES), jnp.int32)
    for e in range(blocks):
        offsets = jnp.where(row // share % blocks == e, shift_ref[0, e] + SMAX, offsets)
        shift_out[e] = jnp.full((MINI, LANES), shift_ref[0, e] + SMAX, jnp.int32)
    shift_out[blocks] = offsets
    count = cols // LANES
    tall_lane = lax.broadcasted_iota(jnp.int32, (block_rows, LANES), 1)
    plans = [sources(shift_ref[0, e] + SMAX, tall_lane, cols) for e in range(blocks)]
    copies[4].wait()
    for e in range(blocks):
        lanes, index = plans[e]
        for c in range(2):
            lines = pl.ds(e * block_rows, block_rows)
            taken = [
                [
                    jnp.take_along_axis(tile_ref[c, lines, v * LANES : (v + 1) * LANES], lanes[odd], axis=1)
                    for v in range(count)
                ]
                for odd in range(2)
            ]
            for b in range(count):
                value = jnp.zeros((block_rows, LANES), jnp.float32)
                low = b % (count // 2) * 2
                for v in range(max(low, 1), min(low + 3, count) + 1):
                    value = jnp.where(index[b] == v, taken[b // (count // 2)][v - 1], value)
                at = b * tall + (c * blocks + e) * share
                for q in range(MINI):
                    packed_ref[pl.ds(slots[q] * height + at, share), :] = value[q * share : (q + 1) * share]
    rest = tails(
        lambda c, e: tile_ref[c, e * block_rows : (e + 1) * block_rows, cols - LANES : cols],
        lambda e: shift_ref[0, e] + SMAX,
        count, tall_lane, cols, blocks, share,
    )
    for q in range(MINI):
        packed_ref[pl.ds(slots[q] * height + count * tall, 1), :] = rest[q * share : q * share + 1]


def rim_kernel(slot_ref, shift_ref, other_ref, packed_ref, out_ref):
    _, rows, cols = other_ref.shape
    blocks = shift_ref.shape[0] - 1
    block_rows = rows // blocks
    share = block_rows // MINI
    tall = 2 * blocks * share
    height = packed_ref.shape[0] // MINI
    count = cols // LANES
    first = lax.axis_index("strip") == 0
    lane = lax.broadcasted_iota(jnp.int32, (MINI, LANES), 1)
    tall_lane = lax.broadcasted_iota(jnp.int32, (block_rows, LANES), 1)
    rim_of, shift_of, moved = {}, [], []
    for e in range(blocks):
        shift_of.append(jnp.concatenate([shift_ref[e]] * (block_rows // MINI), axis=0))
    for c in range(2):
        for e in range(blocks):
            lines = pl.ds(e * block_rows, block_rows)
            rim = jnp.where(first, other_ref[c, lines, 0:LANES], other_ref[c, lines, cols - LANES : cols])
            lanes, _ = sources(shift_of[e], tall_lane, cols)
            moved.append([jnp.take_along_axis(rim, lanes[odd], axis=1) for odd in range(2)])
            rim_of[c, e] = rim
    pieces = [
        [jnp.concatenate([m[odd][q * share : (q + 1) * share] for m in moved], axis=0) for q in range(MINI)]
        for odd in range(2)
    ]
    _, index = sources(shift_ref[blocks], lane, cols)
    wanted = jnp.where(first, count + 1, 0)
    block = jnp.where(first, count // 2 - 1, 0)
    masks = [index[odd * (count // 2)] + 2 * block == wanted for odd in range(2)]
    rest = tails(
        lambda c, e: rim_of[c, e], lambda e: shift_of[e], wanted, tall_lane, cols, blocks, share
    )
    slot = lax.broadcasted_iota(jnp.int32, (MINI, LANES), 0)
    ends = jnp.zeros((MINI, LANES), jnp.float32)
    for q in range(MINI):
        ends = jnp.where(slot == slot_ref[q], rest[q * share : q * share + 1], ends)
    for j in range(MINI):
        rims = [pieces[odd][0] for odd in range(2)]
        for q in range(1, MINI):
            hit = slot_ref[q] == j
            rims = [jnp.where(hit, pieces[odd][q], rims[odd]) for odd in range(2)]
        for odd in range(2):
            at = pl.ds(j * height + (odd * (count // 2) + block) * tall, tall)
            out_ref[at, :] = jnp.where(masks[odd], rims[odd], packed_ref[at, :])
        at = slice((j + 1) * height - 1, (j + 1) * height)
        out_ref[at, :] = packed_ref[at, :] + ends[j : j + 1]


def partner(value, stride):
    places = [ORDER.index(member ^ stride) for member in ORDER]
    return jnp.take_along_axis(value, table(places, value.shape), axis=0)


def link_kernel(tap_ref, coef_ref, data_ref, out_ref):
    blocks = 2
    nb = 2 * out_ref.shape[2] // blocks // LANES
    tall = 4 * blocks
    stride = nb * tall + 1
    lane = lax.broadcasted_iota(jnp.int32, (MINI, LANES), 1)
    by_date = table([ORDER.index(d) for d in range(MINI)], (MINI, LANES))

    def load(row):
        return data_ref[pl.ds(row, MINI, stride=stride), :]

    def sums_of(e, h):
        sums = None
        ends = load(nb * tall)
        for p in range(2):
            pieces = []
            for c in range(2):
                row = (c * blocks + e) * 2 + p
                for odd in range(2):
                    block = odd * (nb // 2) + h
                    if h + 1 < nb // 2:
                        there = load((block + 1) * tall + row)
                    else:
                        there = pltpu.roll(ends, (LANES - (2 * row + odd) * REACH) % LANES, 1)
                    pieces.append((load(block * tall + row), there))
            cache = {}

            def at(c, l):
                m, odd = l // 2, l % 2
                if (c, l) not in cache:
                    here, there = pieces[2 * c + odd]
                    if m:
                        here = pltpu.roll(jnp.where(lane < m, there, here), LANES - m, 1)
                    cache[c, l] = here
                return cache[c, l]

            centre = [[at(c, REACH + odd) for c in range(2)] for odd in range(2)]
            acc = [
                [[tap_ref[0] * centre[odd][c] for c in range(2)] for _ in range(ROUNDS)] for odd in range(2)
            ]
            for k in range(1, REACH + 1):
                for odd in range(2):
                    plus = [at(c, REACH + odd + k) for c in range(2)]
                    minus = [tap_ref[k] * at(c, REACH + odd - k) for c in range(2)]
                    even = [plus[c] + minus[c] for c in range(2)]
                    diff = [plus[c] - minus[c] for c in range(2)]
                    for r in range(ROUNDS):
                        j = r * REACH + k - 1
                        cosine, sine = coef_ref[2 * j], coef_ref[2 * j + 1]
                        total = acc[odd][r]
                        total[0] = total[0] + (cosine * even[0] - sine * diff[1])
                        total[1] = total[1] + (cosine * even[1] + sine * diff[0])
            for odd in range(2):
                terms = []
                for r in range(ROUNDS):
                    y_re, y_im = acc[odd][r]
                    z_re, z_im = partner(y_re, 1 << r), partner(y_im, 1 << r)
                    terms.append(y_re * z_re + y_im * z_im)
                    terms.append(y_im * z_re - y_re * z_im)
                terms.append(centre[odd][0] * centre[odd][0] + centre[odd][1] * centre[odd][1])
                sums = terms if sums is None else [s + t for s, t in zip(sums, terms)]
        return sums

    def energy_of(re, im):
        return jnp.sum(re * re + im * im, axis=0, keepdims=True)

    def shrink(length):
        return 1.0 / jnp.maximum(length, 1.0)

    for g in range(blocks * nb // 2):
        field = sums_of(g // (nb // 2), g % (nb // 2))
        field[-1] = field[-1] * 0.25
        vec_re = field[-1] + (field[0] + field[2] + field[4])
        vec_im = field[1] + field[3] + field[5]
        energies = [energy_of(vec_re, vec_im)]
        for _ in range(1, ITERS):
            next_re = field[-1] * vec_re
            next_im = field[-1] * vec_im
            for r in range(ROUNDS):
                o_re, o_im = partner(vec_re, 1 << r), partner(vec_im, 1 << r)
                t_re, t_im = field[2 * r], field[2 * r + 1]
                next_re = next_re + (t_re * o_re - t_im * o_im)
                next_im = next_im + (t_re * o_im + t_im * o_re)
            vec_re, vec_im = next_re, next_im
            energies.append(energy_of(vec_re, vec_im))
        factor = 1.0
        for energy in energies:
            factor = factor * shrink(jnp.sqrt(energy) * factor)
        for c, vec in enumerate((vec_re, vec_im)):
            out_ref[c, :, pl.ds(g * LANES, LANES)] = jnp.take_along_axis(vec * factor, by_date, axis=0)


def to_owners(linked, inverse, blocks):
    date_count = lax.axis_size("date")
    position = lax.axis_index("date")
    parts = date_count // MINI
    member = position % MINI
    cut = linked.reshape(2, MINI, blocks, parts, -1)
    own_blocks = lax.dynamic_slice_in_dim(jnp.argsort(inverse), member * parts, parts)
    outgoing = jnp.zeros((date_count, 2, MINI, blocks, cut.shape[-1]), jnp.float32)
    outgoing = outgoing.at[own_blocks].set(jnp.moveaxis(cut, 3, 0))
    arrived = lax.all_to_all(outgoing, "date", split_axis=0, concat_axis=0, tiled=True)
    source = inverse[position] // parts
    arrived = arrived.reshape((parts, MINI) + arrived.shape[1:])
    chosen = lax.dynamic_index_in_dim(arrived, source, axis=1, keepdims=False)
    return jnp.moveaxis(chosen, 1, 0).reshape(2, date_count, -1)


def shards(slc_tiles, coreg_shift, center_freq, filter_taps, owner_table):
    own_tile = slc_tiles[:, 0]
    _, rows, cols = own_tile.shape
    date_count = lax.axis_size("date")
    strips = lax.axis_size("strip")
    blocks = coreg_shift.shape[1]
    share = rows // blocks // MINI
    position = lax.axis_index("date")
    other_tile = lax.ppermute(own_tile, "strip", [(s, strips - 1 - s) for s in range(strips)])
    if date_count == MINI:
        slots, freq = owner_table, center_freq
    else:
        slots = jnp.arange(MINI, dtype=jnp.int32)
        freq = lax.dynamic_slice_in_dim(center_freq, position // MINI * MINI, MINI)
    tall = 2 * blocks * share
    height = tall * (cols // LANES) + 1
    tile = (MINI, LANES)
    coefs, taps, slot_marks, shift_marks, packed = pl.pallas_call(
        prep_kernel,
        out_shape=(
            jax.ShapeDtypeStruct((2 * ROUNDS * REACH,) + tile, jnp.float32),
            jax.ShapeDtypeStruct((REACH + 1,) + tile, jnp.float32),
            jax.ShapeDtypeStruct((MINI,) + tile, jnp.int32),
            jax.ShapeDtypeStruct((blocks + 1,) + tile, jnp.int32),
            jax.ShapeDtypeStruct((MINI * height, LANES), jnp.float32),
        ),
        in_specs=[hbm()] * 5,
        out_specs=(vmem(),) * 5,
        scratch_shapes=[
            pltpu.SMEM(freq.shape, jnp.float32),
            pltpu.SMEM(filter_taps.shape, jnp.float32),
            pltpu.SMEM(slots.shape, jnp.int32),
            pltpu.SMEM(coreg_shift.shape, jnp.int32),
            pltpu.VMEM(own_tile.shape, jnp.float32),
            pltpu.SemaphoreType.DMA((5,)),
        ],
        compiler_params=params(),
        name="prep",
    )(*(in_hbm(x) for x in (freq, filter_taps, slots, coreg_shift, own_tile)))
    packed = pl.pallas_call(
        rim_kernel,
        out_shape=jax.ShapeDtypeStruct(packed.shape, jnp.float32),
        in_specs=[vmem()] * 4,
        out_specs=vmem(),
        input_output_aliases={3: 0},
        compiler_params=params(),
        name="rim",
    )(slot_marks, shift_marks, other_tile, packed)
    stacks = [[g + member for member in ORDER] for g in range(0, date_count, MINI)]
    data = lax.all_to_all(
        packed.reshape(MINI, 1, height * LANES), "date", split_axis=0, concat_axis=0, axis_index_groups=stacks, tiled=True
    )
    linked = pl.pallas_call(
        link_kernel,
        out_shape=jax.ShapeDtypeStruct((2, MINI, blocks * share // 2 * cols // 2), jnp.float32),
        in_specs=[vmem()] * 3,
        out_specs=vmem(),
        compiler_params=params(),
        name="link",
    )(taps, coefs, data.reshape(-1, LANES))
    if date_count == MINI:
        return linked
    date_ids = jnp.arange(date_count, dtype=jnp.int32)
    inverse = jnp.zeros((date_count,), jnp.int32).at[owner_table].set(date_ids)
    return to_owners(linked, inverse, blocks)


def solution(mesh):
    in_specs = (
        P(None, ("groups", "date"), None, "strip"),
        P(("groups", "date"), None),
        P("groups"),
        P(),
        P("groups"),
    )
    out_specs = P(None, "groups", ("date", "strip"))
    return jax.shard_map(shards, mesh=mesh, in_specs=in_specs, out_specs=out_specs, check_vma=False)
```
